32 devices in a mesh: groups: 2 (over y), section: 4 (over z), dp: 4 (over x, core).
Axes of the slice: x: 2, y: 2, z: 4, core: 2. Of those that a mesh axis runs over, the one named last changes fastest.
Arguments:
- stream_in: bfloat16 [1152, 3072], P(('groups', 'dp')), parts along dimension 0, may hold values from -6 to 6
- out_grad: bfloat16 [1152, 3072], P(('groups', 'dp')), parts along dimension 0, may hold values from -6 to 6
- mask_blocks: int32 [24, 3, 3], P(('groups', 'dp')), parts along dimension 0, may hold values from 0 to 2, as said below
- norm_gain: float32 [4, 3072], P('section'), may hold values from 0.4 to 1.6
- w_joined: bfloat16 [4, 3072, 1664], P('section', 'dp'), may hold values from -0.109375 to 0.109375
- w_out: bfloat16 [4, 1536, 3072], P('section', 'dp'), may hold values from -0.15625 to 0.15625
Outputs:
- grad_joined: float32 [8, 3072, 1664], P(('groups', 'section'), 'dp'), parts along dimension 0
- grad_out: float32 [8, 1536, 3072], P(('groups', 'section'), 'dp'), parts along dimension 0
- gain_grad: float32 [8, 3072], P(('groups', 'section')), parts along dimension 0
The draws below stay inside these ranges and needn't reach their ends.
There are 2 independent parts, one for each index of `groups`. The reference program is written for one: setup_inputs(seed, part) draws one part's arguments, and reference() takes and returns one part's arrays. A program takes and returns all parts, laid end to end along the dimension named above; an argument that names none is the same for every part. Nothing has to cross between parts.
Inputs may be any that keep to these rules, and one draw needn't show every extreme that they name: `mask_blocks`: entry 0 of the list of query block i is i itself.
All inputs are finite; a program needn't handle non-finite values.
Results may differ from the reference program's by a relative error of at most 0.024.
Values may be sent and summed in bfloat16 or wider, within the bound.
A program may use at most 128 MiB of HBM per device.

```python
import jax
import jax.numpy as jnp
from jax import lax

MODEL_DIM = 3072
NUM_HEADS = 24
HEAD_DIM = 64
MICRO_LEN = 48
BLOCK_LEN = 16
INNER_DIM = 1536
JOINED_DIM = 1664
NUM_BLOCKS = 3
SECTIONS = 4
MICRO_ALL = 12
TOKENS = 576
N_DP = 4


def draw_mask_blocks(key, part):
    base = jax.random.fold_in(key, 17)
    side_key, stripe_key = jax.random.split(base)
    own_block = jnp.broadcast_to(jnp.arange(NUM_BLOCKS, dtype=jnp.int32)[None, :], (MICRO_ALL, NUM_BLOCKS))
    side_step = jax.random.randint(side_key, (MICRO_ALL, NUM_BLOCKS), 0, 2).astype(jnp.int32) * 2 - 1
    near_block = jnp.clip(own_block + side_step, 0, NUM_BLOCKS - 1)
    stripe_block = jax.random.randint(stripe_key, (MICRO_ALL, NUM_BLOCKS), 0, NUM_BLOCKS).astype(jnp.int32)
    return jnp.stack([own_block, near_block, stripe_block], axis=-1).astype(jnp.int32)


def shard_levels(own_key, extent, cuts, smallest, top_value):
    def one(dim, blocks):
        heights = jax.random.uniform(jax.random.fold_in(jax.random.fold_in(own_key, 6), dim), (blocks,), jnp.float32, smallest / len(cuts), top_value / len(cuts))
        return jnp.repeat(jnp.exp(heights), extent[dim] // blocks).reshape((-1,) + (1,) * (len(extent) - dim - 1))

    factor_of = one(*cuts[0])
    for cut in cuts[1:]:
        factor_of = factor_of * one(*cut)
    return factor_of


def noise(key, dims, deviation, limit, pieces=(), held_as=jnp.bfloat16):
    values = jax.random.normal(key, dims, jnp.float32) * deviation
    if len(pieces) > 0:
        values = shard_levels(key, dims, pieces, -0.22, 0.18) * values
    return jnp.clip(values, min=-limit, max=limit).astype(held_as)


def setup_inputs(seed: int = 0, part: int = 0) -> dict:
    key_list = jax.random.split(jax.random.key(seed), 7)
    part_splits = jax.random.split(jax.random.fold_in(key_list[6], part), 7)
    return {
        "stream_in": noise(part_splits[0], (TOKENS, MODEL_DIM), 1.0, 6.0, ((0, 4),)),
        "out_grad": noise(part_splits[1], (TOKENS, MODEL_DIM), 1.0, 6.0, ((0, 4),)),
        "mask_blocks": draw_mask_blocks(jax.random.fold_in(jax.random.fold_in(key_list[6], part), 71), part),
        "norm_gain": jnp.clip(1.0 + 0.12 * jax.random.normal(key_list[3], (SECTIONS, MODEL_DIM), jnp.float32), 0.4, 1.6),
        "w_joined": noise(key_list[4], (SECTIONS, MODEL_DIM, JOINED_DIM), MODEL_DIM ** -0.5, 0.109375, ((0, 4), (1, 4))),
        "w_out": noise(key_list[5], (SECTIONS, INNER_DIM, MODEL_DIM), INNER_DIM ** -0.5, 0.15625, ((0, 4), (1, 4))),
    }


EPSILON = 1e-05

def allowed_tokens(links, block_len):
    count = links.shape[1]
    block_hits = links[:, :, :, None] == jnp.arange(count, dtype=jnp.int32)[None, None, None, :]
    blocks = jnp.any(block_hits, axis=2)
    return jnp.repeat(jnp.repeat(blocks, block_len, axis=1), block_len, axis=2)

def normalize(stream, gain_row):
    stream_wide = stream.astype(jnp.float32)
    inv_rms = lax.rsqrt(lax.optimization_barrier(jnp.mean(stream_wide * stream_wide, axis=-1, keepdims=True)) + EPSILON)
    normed = (stream_wide * inv_rms * gain_row).astype(jnp.bfloat16)
    return (stream_wide, inv_rms, normed)

def project(normed, weight):
    batch_size, length, model_width = normed.shape
    flat = jnp.dot(normed.reshape(-1, model_width), weight, preferred_element_type=jnp.float32)
    return flat.astype(jnp.bfloat16).reshape(batch_size, length, weight.shape[1])

def attend(joined_rows, allowed):
    batch_size, length, _ = joined_rows.shape
    inner_width = NUM_HEADS * HEAD_DIM
    queries = joined_rows[:, :, :inner_width].reshape(batch_size, length, NUM_HEADS, HEAD_DIM)
    key_rows = joined_rows[:, :, inner_width:inner_width + HEAD_DIM]
    values = joined_rows[:, :, inner_width + HEAD_DIM:]
    scores = jnp.einsum('bihd,bjd->bhij', queries.astype(jnp.float32), key_rows.astype(jnp.float32)) * HEAD_DIM ** (-0.5)
    scores = jnp.where(allowed[:, None], scores, -1e+30)
    row_max = lax.optimization_barrier(jnp.max(scores, axis=-1, keepdims=True))
    exp_scores = jnp.exp(scores - row_max)
    attn_probs = exp_scores / lax.optimization_barrier(jnp.sum(exp_scores, axis=-1, keepdims=True))
    probs_half = attn_probs.astype(jnp.bfloat16)
    mixed_heads = jnp.einsum('bhij,bjd->bihd', probs_half.astype(jnp.float32), values.astype(jnp.float32))
    mixed_heads = mixed_heads.astype(jnp.bfloat16).reshape(batch_size, length, inner_width)
    return (queries, key_rows, values, attn_probs, probs_half, mixed_heads)

def layer_forward(stream, gain_row, w_joined, w_out, allowed):
    stream_wide, inv_rms, normed = normalize(stream, gain_row)
    joined_rows = project(normed, w_joined)
    mixed_heads = attend(joined_rows, allowed)[5]
    batch_size, length, model_width = stream.shape
    update = jnp.dot(mixed_heads.reshape(-1, mixed_heads.shape[2]), w_out, preferred_element_type=jnp.float32)
    return (stream_wide + update.reshape(batch_size, length, model_width)).astype(jnp.bfloat16)

def layer_backward(stream, gain_row, joined_rows, w_joined, w_out, allowed, upstream):
    stream_wide, inv_rms, normed = normalize(stream, gain_row)
    queries, key_rows, values, attn_probs, probs_half, mixed_heads = attend(joined_rows, allowed)
    batch_size, length, model_width = stream.shape
    inner_width = NUM_HEADS * HEAD_DIM
    grad_mixed = lax.dot_general(upstream.reshape(-1, model_width), w_out, (((1,), (1,)), ((), ())), preferred_element_type=jnp.float32)
    grad_mixed = grad_mixed.astype(jnp.bfloat16).reshape(batch_size, length, NUM_HEADS, HEAD_DIM)
    grad_probs = jnp.einsum('bihd,bjd->bhij', grad_mixed.astype(jnp.float32), values.astype(jnp.float32))
    grad_values = jnp.einsum('bhij,bihd->bjd', probs_half.astype(jnp.float32), grad_mixed.astype(jnp.float32))
    inner_sum = lax.optimization_barrier(jnp.sum(attn_probs * grad_probs, axis=-1, keepdims=True))
    grad_scores = (attn_probs * (grad_probs - inner_sum) * HEAD_DIM ** (-0.5)).astype(jnp.bfloat16)
    grad_queries = jnp.einsum('bhij,bjd->bihd', grad_scores.astype(jnp.float32), key_rows.astype(jnp.float32))
    grad_keys = jnp.einsum('bhij,bihd->bjd', grad_scores.astype(jnp.float32), queries.astype(jnp.float32))
    grad_joined_rows = jnp.concatenate([grad_queries.reshape(batch_size, length, inner_width), grad_keys, grad_values], axis=-1).astype(jnp.bfloat16)
    grad_normed = lax.dot_general(grad_joined_rows.reshape(-1, grad_joined_rows.shape[2]), w_joined, (((1,), (1,)), ((), ())), preferred_element_type=jnp.float32)
    grad_normed = grad_normed.reshape(batch_size, length, model_width)
    gained = grad_normed * gain_row
    grad_stream = inv_rms * gained - stream_wide * inv_rms ** 3 * lax.optimization_barrier(jnp.mean(stream_wide * gained, axis=-1, keepdims=True))
    down_grad = (upstream.astype(jnp.float32) + grad_stream).astype(jnp.bfloat16)
    gain_part = lax.optimization_barrier(jnp.sum((grad_normed * stream_wide * inv_rms).reshape(-1, model_width), axis=0))
    return (down_grad, normed, grad_joined_rows, mixed_heads, gain_part)

def replica_sum(left, right):
    left_rows = left.reshape(N_DP, -1, left.shape[-1]).astype(jnp.float32)
    right_rows = right.reshape(N_DP, -1, right.shape[-1]).astype(jnp.float32)
    partial_sums = jnp.einsum('rtd,rtc->rdc', left_rows, right_rows)
    rounded = lax.optimization_barrier(partial_sums.astype(jnp.bfloat16))
    return lax.optimization_barrier(jnp.sum(rounded.astype(jnp.float32), axis=0))

def reference(stream_in, out_grad, mask_blocks, norm_gain, w_joined, w_out):
    allowed = allowed_tokens(mask_blocks, BLOCK_LEN)
    micro_count = mask_blocks.shape[0]
    model_width = stream_in.shape[1]
    current = stream_in.reshape(micro_count, MICRO_LEN, model_width)
    inputs_kept = []
    for section_index in range(SECTIONS):
        inputs_kept.append(current)
        current = layer_forward(current, norm_gain[section_index], w_joined[section_index], w_out[section_index], allowed)
    upstream = out_grad.reshape(micro_count, MICRO_LEN, model_width)
    joined_list = [None] * SECTIONS
    out_list = [None] * SECTIONS
    gain_list = [None] * SECTIONS
    for section_index in reversed(range(SECTIONS)):
        source = inputs_kept[section_index]
        normed = normalize(source, norm_gain[section_index])[2]
        joined_rows = project(normed, w_joined[section_index])
        down_grad, normed, grad_joined_rows, mixed_heads, gain_part = layer_backward(source, norm_gain[section_index], joined_rows, w_joined[section_index], w_out[section_index], allowed, upstream)
        joined_list[section_index] = replica_sum(normed, grad_joined_rows)
        out_list[section_index] = replica_sum(mixed_heads, upstream)
        gain_list[section_index] = gain_part
        upstream = down_grad
    return (jnp.stack(joined_list), jnp.stack(out_list), jnp.stack(gain_list))
```

```python
import functools
import types

import jax
import jax.numpy as jnp
from jax import lax
from jax.experimental import pallas as pl
from jax.experimental.pallas import tpu as pltpu
from jax.sharding import PartitionSpec as P

HEAD_DIM = 64
BLOCK_LEN = 16
LANES = 128
CORES = 2
EPSILON = 1e-05
F32 = jnp.float32
BF16 = jnp.bfloat16
NN = (((1,), (0,)), ((), ()))
NT = (((1,), (1,)), ((), ()))
TN = (((0,), (0,)), ((), ()))

LAG = dict(F0=0, F1=0, F2=1, F3=1, F4=2, B0=0, BR=0, B1=1, GR=1, B3=2)
ORDER = ("F0", "B0", "F2", "F4", "BR", "F1", "F3", "B1", "GR", "B3")
FIRST_BACK = 1
STAGE_GAP = LAG["F4"] + LAG["B3"] + 2


def dot(left, right, dims=NN):
    return lax.dot_general(left, right, dims, preferred_element_type=F32)


def step_kernel(d, stream, ograd, bias, gain, wj, wo, gj_out, go_out, gain_out, *scratch):
    s = types.SimpleNamespace(**dict(zip(d.names, scratch)))
    n, k, T, F, H, W, chips = d.n, d.k, d.T, d.F, d.H, d.W, d.chips
    me = lax.axis_index("dp")
    sec = lax.axis_index("section")
    last = d.S - 1
    chip, core = me // CORES, lax.rem(me, CORES)
    sib = me + 1 - 2 * core
    others = range(1, chips)

    def ahead(kk):
        return lax.rem(chip + kk, chips) * CORES

    def behind(kk):
        return lax.rem(chip + chips - kk, chips) * CORES

    def push(src, dst, send, recv, device):
        pltpu.make_async_remote_copy(
            src_ref=src,
            dst_ref=dst,
            send_sem=send,
            recv_sem=recv,
            device_id=device,
            device_id_type=pl.DeviceIdType.MESH,
        ).start()

    def done(ref, sem):
        pltpu.make_async_copy(ref, ref, sem).wait()

    def cols(index, width):
        return pl.ds(pl.multiple_of(index * width, LANES), width)

    to_sib = {"dp": sib}

    def column(kk):
        return pl.ds(0, H) if kk == 0 else pl.ds(W + (kk - 1) * H, H)

    def pieces(which):
        out = []
        for kk in range(chips):
            e = ahead(kk) + which
            out.append((wj, cols(e, H), s.wjf, column(kk)))
        out.append((wj, pl.ds(n * H, W - H), s.wjf, pl.ds(H, W - H)))
        for kk in range(chips):
            e = ahead(kk) + which
            out.append((wo, cols(e, F), s.wof, pl.ds(kk * F, F)))
        return out

    loads = []
    for i, (src, there, dst, here) in enumerate(pieces(core)):
        rows = src.shape[0]
        loads.append(
            pltpu.make_async_copy(
                src.at[:, there], dst.at[pl.ds(0, rows), here], s.w_l.at[i]
            )
        )
    loads.append(pltpu.make_async_copy(wj, s.wj_own, s.w_l.at[2 * chips + 1]))
    loads.append(pltpu.make_async_copy(wo, s.wo_own, s.w_l.at[2 * chips + 2]))
    for copy in loads:
        copy.start()

    barrier = pltpu.get_barrier_semaphore()

    def greet(device):
        pl.semaphore_signal(
            barrier, inc=1, device_id=device, device_id_type=pl.DeviceIdType.MESH
        )

    for shift in range(1, n):
        greet({"dp": lax.rem(me + shift, n)})

    @pl.when(sec > 0)
    def _():
        greet({"section": sec - 1})

    @pl.when(sec < last)
    def _():
        greet({"section": sec + 1})

    pl.semaphore_wait(
        barrier, n - 1 + (sec > 0).astype(jnp.int32) + (sec < last).astype(jnp.int32)
    )

    def spread(source, target, send, recv):
        for i in range(d.mb):
            t = i * n + me
            rows = pl.ds(i * T, T)
            pltpu.make_async_copy(source.at[rows, cols(me, F)], target(t), recv.at[t]).start()
            for shift in range(1, n):
                e = lax.rem(me + shift, n)
                push(
                    source.at[rows, cols(e, F)],
                    target(t),
                    send.at[i, shift - 1],
                    recv.at[t],
                    {"dp": e},
                )

    def spread_sent(source, send):
        for i in range(d.mb):
            for shift in range(1, n):
                e = lax.rem(me + shift, n)
                done(source.at[pl.ds(i * T, T), cols(e, F)], send.at[i, shift - 1])

    @pl.when(sec == 0)
    def _():
        spread(stream, lambda t: s.x_own.at[t], s.d_s, s.x_r)

    for i, (src, there, dst, here) in enumerate(pieces(1 - core)):
        rows = src.shape[0]
        push(
            src.at[:, there],
            dst.at[pl.ds(rows, rows), here],
            s.w_s.at[i],
            s.w_r.at[i],
            to_sib,
        )

    own_bias = pltpu.make_async_copy(bias, s.bias_all.at[me], s.w_l.at[2 * chips + 3])
    own_bias.start()
    for shift in range(1, n):
        e = lax.rem(me + shift, n)
        push(bias, s.bias_all.at[me], s.b_s.at[shift - 1], s.b_r.at[shift - 1], {"dp": e})

    @pl.when(sec == last)
    def _():
        for i in range(d.mb):
            t = i * n + me
            rows = pl.ds(i * T, T)
            pltpu.make_async_copy(
                ograd.at[rows, cols(me, F)], s.u_all.at[me, t], s.u_r.at[t]
            ).start()
            for shift in range(1, n):
                e = lax.rem(me + shift, n)
                push(
                    ograd.at[rows, cols(e, F)],
                    s.u_all.at[e, t],
                    s.g_s.at[i, shift - 1],
                    s.u_r.at[t],
                    {"dp": e},
                )

    s.gain_acc[...] = jnp.zeros_like(s.gain_acc)
    for copy in loads:
        copy.wait()
    own_bias.wait()
    for i, (src, there, dst, here) in enumerate(pieces(core)):
        rows = src.shape[0]
        done(dst.at[pl.ds(rows, rows), here], s.w_r.at[i])
    for shift in range(1, n):
        done(s.bias_all.at[lax.rem(me + n - shift, n)], s.b_r.at[shift - 1])

    def eye():
        return lax.broadcasted_iota(jnp.int32, (T, LANES), 0) == lax.broadcasted_iota(
            jnp.int32, (T, LANES), 1
        )

    def to_row(column_values):
        return jnp.sum(jnp.where(eye(), column_values, 0.0), axis=0, keepdims=True)

    def to_column(row_values):
        return jnp.sum(
            jnp.where(eye(), jnp.broadcast_to(row_values, (T, LANES)), 0.0), axis=1, keepdims=True
        )

    def low_half(rows):
        return lax.broadcasted_iota(jnp.int32, (rows, LANES), 1) < HEAD_DIM

    def stack_heads(rows):
        low = low_half(T)
        out = []
        for pair in range(H // LANES):
            both = rows[:, pair * LANES : (pair + 1) * LANES]
            out += [jnp.where(low, both, 0.0), jnp.where(low, 0.0, both)]
        return jnp.concatenate(out, axis=0)

    def unstack_heads(rows):
        low = low_half(T)
        out = []
        for pair in range(H // LANES):
            first = rows[2 * pair * T : (2 * pair + 1) * T]
            second = rows[(2 * pair + 1) * T : (2 * pair + 2) * T]
            out.append(jnp.where(low, first, second))
        return jnp.concatenate(out, axis=1)

    def doubled(kv):
        low = low_half(T)
        turned = pltpu.roll(kv, HEAD_DIM, 1)
        return jnp.where(low, kv, turned).astype(BF16), jnp.where(low, turned, kv).astype(BF16)

    g_own = gain[:, cols(me, F)]
    g_sib = gain[:, cols(sib, F)]

    def f0(t):
        done(s.x_own.at[t], s.x_r.at[t])
        push(s.x_own.at[t], s.x_sib.at[t], s.xs_s.at[t], s.xs_r.at[t], to_sib)

    def f1(t):
        own = s.x_own[t].astype(F32)
        done(s.x_sib.at[t], s.xs_r.at[t])
        beside = s.x_sib[t].astype(F32)
        squares = jnp.sum(own * own, axis=1, keepdims=True) + jnp.sum(
            beside * beside, axis=1, keepdims=True
        )
        part = dot((own * g_own).astype(BF16), s.wjf[:F]) + dot(
            (beside * g_sib).astype(BF16), s.wjf[F:]
        )
        s.j_own[t] = part[:, :W]
        s.st_own[t] = to_row(squares)
        for kk in others:
            s.j_send[kk - 1, t, :, :H] = part[:, W + (kk - 1) * H : W + kk * H].astype(BF16)
            s.j_send[kk - 1, t, :, H:] = part[:, H:W].astype(BF16)
        for kk in others:
            there = {"dp": ahead(kk) + core}
            at = (kk - 1, t)
            push(s.j_send.at[at], s.j_recv.at[at], s.j_s.at[at], s.j_r.at[at], there)
            push(s.st_own.at[t], s.st_recv.at[at], s.st_s.at[at], s.st_r.at[at], there)
        done(s.x_own.at[t], s.xs_s.at[t])

    def f2(t):
        total = s.j_own[t]
        squares = s.st_own[t]
        for kk in others:
            at = (kk - 1, t)
            done(s.j_recv.at[at], s.j_r.at[at])
            done(s.st_recv.at[at], s.st_r.at[at])
            total = total + s.j_recv[at].astype(F32)
            squares = squares + s.st_recv[at]
        inv_rms = lax.rsqrt(to_column(squares) / d.D + EPSILON)
        joined = (total * inv_rms).astype(BF16)
        s.qkv[t] = joined
        s.r_all[t] = jnp.broadcast_to(inv_rms, (T, LANES))
        wide = joined.astype(F32)
        queries = stack_heads(wide[:, :H]).astype(BF16)
        kk_rows, vv_rows = doubled(wide[:, H:])
        scores = dot(queries, kk_rows, NT) * HEAD_DIM ** (-0.5)
        blocks = s.bias_all[lax.rem(t, n), t // n]
        rows = [
            jnp.broadcast_to(blocks[b : b + 1, :T], (BLOCK_LEN, T)) for b in range(T // BLOCK_LEN)
        ]
        scores = scores + jnp.concatenate(rows * (H // HEAD_DIM), axis=0)
        exps = jnp.exp(scores - jnp.max(scores, axis=1, keepdims=True))
        probs = exps / jnp.sum(exps, axis=1, keepdims=True)
        s.probs[t] = probs
        s.mixed[t] = unstack_heads(dot(probs.astype(BF16), vv_rows)).astype(BF16)

        @pl.when(sec < last)
        def _():
            push(s.mixed.at[t], s.mixed_sib.at[t], s.m_s.at[t], s.m_r.at[t], to_sib)

        for kk in others:
            at = (kk - 1, t)
            done(s.j_send.at[at], s.j_s.at[at])
            done(s.st_own.at[t], s.st_s.at[at])

    def f3(t):
        @pl.when(sec < last)
        def _():
            done(s.mixed_sib.at[t], s.m_r.at[t])
            part = dot(s.mixed[t], s.wof[:H]) + dot(s.mixed_sib[t], s.wof[H:])
            for kk in others:
                at = (kk - 1, t)
                s.y_send[at] = part[:, kk * F : (kk + 1) * F].astype(BF16)
                push(
                    s.y_send.at[at],
                    s.y_recv.at[at],
                    s.y_s.at[at],
                    s.y_r.at[at],
                    {"dp": ahead(kk) + core},
                )
            s.y_own[t] = part[:, :F] + s.x_own[t].astype(F32)
            done(s.mixed.at[t], s.m_s.at[t])

    def f4(t):
        @pl.when(sec < last)
        def _():
            total = s.y_own[t]
            for kk in others:
                at = (kk - 1, t)
                done(s.y_recv.at[at], s.y_r.at[at])
                total = total + s.y_recv[at].astype(F32)
            s.z_send[t] = total.astype(BF16)
            push(s.z_send.at[t], s.x_own.at[t], s.z_s.at[t], s.x_r.at[t], {"section": sec + 1})
            for kk in others:
                at = (kk - 1, t)
                done(s.y_send.at[at], s.y_s.at[at])

    def b0(t):
        mine = s.u_all.at[me, t]
        done(mine, s.u_r.at[t])
        for kk in others:
            at = (kk - 1, t)
            push(mine, mine, s.ux_s.at[at], s.ux_r.at[at], {"dp": ahead(kk) + core})
        push(mine, mine, s.us_s.at[t], s.us_r.at[t], to_sib)

    def br(t):
        for kk in others:
            at = (kk - 1, t)
            block = s.u_all.at[behind(kk) + core, t]
            done(block, s.ux_r.at[at])
            push(block, block, s.ur_s.at[at], s.ur_r.at[at], to_sib)

    def b1(t):
        done(s.u_all.at[sib, t], s.us_r.at[t])
        for kk in others:
            done(s.u_all.at[behind(kk) + 1 - core, t], s.ur_r.at[kk - 1, t])
        upstream = jnp.concatenate([s.u_all[e, t] for e in range(n)], axis=1)
        grad_mixed = dot(upstream, s.wo_own[...], NT).astype(BF16).astype(F32)
        grads = stack_heads(grad_mixed).astype(BF16)
        joined = s.qkv[t].astype(F32)
        queries = stack_heads(joined[:, :H]).astype(BF16)
        kk_rows, vv_rows = doubled(joined[:, H:])
        probs = s.probs[t]
        grad_probs = dot(grads, vv_rows, NT)
        inner = jnp.sum(probs * grad_probs, axis=1, keepdims=True)
        grad_scores = (probs * (grad_probs - inner) * HEAD_DIM ** (-0.5)).astype(BF16)
        grad_values = dot(probs.astype(BF16), grads, TN)
        grad_keys = dot(grad_scores, queries, TN)
        grad_queries = unstack_heads(dot(grad_scores, kk_rows))
        grad_kv = jnp.where(
            low_half(T),
            grad_keys + pltpu.roll(grad_keys, HEAD_DIM, 1),
            grad_values + pltpu.roll(grad_values, HEAD_DIM, 1),
        )
        message = jnp.concatenate([grad_queries, grad_kv], axis=1)
        s.g_all[me, t] = message.astype(BF16)
        s.gs_all[me, t] = to_row(jnp.sum(message * joined, axis=1, keepdims=True))
        mine, stat = s.g_all.at[me, t], s.gs_all.at[me, t]
        for kk in others:
            at = (kk - 1, t)
            there = {"dp": ahead(kk) + core}
            push(mine, mine, s.gx_s.at[at], s.gx_r.at[at], there)
            push(stat, stat, s.hx_s.at[at], s.hx_r.at[at], there)
        push(mine, mine, s.gs_s.at[t], s.gs_r.at[t], to_sib)
        push(stat, stat, s.hs_s.at[t], s.hs_r.at[t], to_sib)
        block = s.u_all.at[me, t]
        done(block, s.us_s.at[t])
        for kk in others:
            at = (kk - 1, t)
            done(block, s.ux_s.at[at])
            done(s.u_all.at[behind(kk) + core, t], s.ur_s.at[at])

    def gr(t):
        for kk in others:
            at = (kk - 1, t)
            e = behind(kk) + core
            block, stat = s.g_all.at[e, t], s.gs_all.at[e, t]
            done(block, s.gx_r.at[at])
            push(block, block, s.gr_s.at[at], s.gr_r.at[at], to_sib)
            done(stat, s.hx_r.at[at])
            push(stat, stat, s.hr_s.at[at], s.hr_r.at[at], to_sib)

    def b3(t):
        done(s.g_all.at[sib, t], s.gs_r.at[t])
        done(s.gs_all.at[sib, t], s.hs_r.at[t])
        for kk in others:
            e = behind(kk) + 1 - core
            done(s.g_all.at[e, t], s.gr_r.at[kk - 1, t])
            done(s.gs_all.at[e, t], s.hr_r.at[kk - 1, t])
        blocks = [s.g_all[e, t] for e in range(n)]
        grad_kv = functools.reduce(lambda a, b: a + b, [b[:, H:].astype(F32) for b in blocks])
        grad_kv = grad_kv.astype(BF16)
        s.gkv[t] = grad_kv
        rows = jnp.concatenate([b[:, :H] for b in blocks] + [grad_kv], axis=1)
        grad_normed = dot(rows, s.wj_own[...], NT)
        stat = functools.reduce(lambda a, b: a + b, [s.gs_all[e, t] for e in range(n)])
        inv_rms = s.r_all[t][:, :1]
        wide = s.x_own[t].astype(F32)
        scaled = wide * inv_rms
        s.normed[t] = (scaled * g_own).astype(BF16)
        s.gain_acc[...] += jnp.sum((grad_normed * scaled).reshape(T // 8, 8, F), axis=0)

        @pl.when(sec > 0)
        def _():
            mean = to_column(stat) / d.D
            down = s.u_all[me, t].astype(F32) + inv_rms * (g_own * grad_normed - scaled * mean)
            s.d_send[t] = down.astype(BF16)
            push(
                s.d_send.at[t], s.u_all.at[me, t], s.dz_s.at[t], s.u_r.at[t], {"section": sec - 1}
            )

        mine, own_stat = s.g_all.at[me, t], s.gs_all.at[me, t]
        done(mine, s.gs_s.at[t])
        done(own_stat, s.hs_s.at[t])
        for kk in others:
            at = (kk - 1, t)
            e = behind(kk) + core
            done(mine, s.gx_s.at[at])
            done(own_stat, s.hx_s.at[at])
            done(s.g_all.at[e, t], s.gr_s.at[at])
            done(s.gs_all.at[e, t], s.hr_s.at[at])

    phases = dict(F0=f0, F1=f1, F2=f2, F3=f3, F4=f4, B0=b0, BR=br, B1=b1, GR=gr, B3=b3)
    gap = jnp.minimum(FIRST_BACK + STAGE_GAP * (last - sec), k + LAG["F4"])

    def step(now, carry):
        for name in ORDER:
            t = now - LAG[name] - (gap if name[0] != "F" else 0)

            @pl.when(jnp.logical_and(t >= 0, t < k))
            def _(name=name, t=t):
                phases[name](t)

        return carry

    lax.fori_loop(0, k + gap + LAG["B3"], step, 0)

    s.gain_all[me] = jnp.sum(s.gain_acc[...], axis=0, keepdims=True)
    for shift in range(1, n):
        push(
            s.gain_all.at[me],
            s.gain_all.at[me],
            s.n_s.at[shift - 1],
            s.n_r.at[shift - 1],
            {"dp": lax.rem(me + shift, n)},
        )
    normed = s.normed[...].reshape(k * T, F)
    mixed = s.mixed[...].reshape(k * T, H)
    outs = []
    for e in range(n):
        s.gj[:, e * H : (e + 1) * H] = dot(normed, s.g_all[e, :, :, :H].reshape(k * T, H), TN)
        here = pl.ds(e * H, H)
        outs.append(pltpu.make_async_copy(s.gj.at[:, here], gj_out.at[:, here], s.o_s.at[2 * e]))
        outs[-1].start()
        s.go[:, e * F : (e + 1) * F] = dot(mixed, s.u_all[e].reshape(k * T, F), TN)
        here = pl.ds(e * F, F)
        outs.append(
            pltpu.make_async_copy(s.go.at[:, here], go_out.at[:, here], s.o_s.at[2 * e + 1])
        )
        outs[-1].start()
    s.gj[:, n * H :] = dot(normed, s.gkv[...].reshape(k * T, W - H), TN)
    here = pl.ds(n * H, W - H)
    outs.append(pltpu.make_async_copy(s.gj.at[:, here], gj_out.at[:, here], s.o_s.at[2 * n]))
    outs[-1].start()

    for shift in range(1, n):
        done(s.gain_all.at[lax.rem(me + n - shift, n)], s.n_r.at[shift - 1])
        done(s.gain_all.at[me], s.n_s.at[shift - 1])
    gain_out[...] = s.gain_all[...]

    @pl.when(sec == 0)
    def _():
        spread_sent(stream, s.d_s)

    @pl.when(sec == last)
    def _():
        spread_sent(ograd, s.g_s)

    for i, (src, there, dst, here) in enumerate(pieces(1 - core)):
        done(src.at[:, there], s.w_s.at[i])
    for shift in range(1, n):
        done(bias, s.b_s.at[shift - 1])

    @pl.when(sec < last)
    def _():
        lax.fori_loop(0, k, lambda t, c: (done(s.z_send.at[t], s.z_s.at[t]), c)[1], 0)

    @pl.when(sec > 0)
    def _():
        lax.fori_loop(0, k, lambda t, c: (done(s.d_send.at[t], s.dz_s.at[t]), c)[1], 0)

    for copy in outs:
        copy.wait()


def train_step(d, stream, ograd, bias, gain, wj, wo):
    n, k, T, F, H, W = d.n, d.k, d.T, d.F, d.H, d.W
    o = d.chips - 1
    J = n * H + W - H
    vmem, dma = pltpu.VMEM, pltpu.SemaphoreType.DMA
    each, cross = dma((k,)), dma((o, k))
    scratch = dict(
        wjf=vmem((2 * F, W + o * H), BF16),
        wof=vmem((2 * H, d.chips * F), BF16),
        wj_own=vmem((F, J), BF16),
        wo_own=vmem((H, d.D), BF16),
        bias_all=vmem((n,) + bias.shape, F32),
        x_own=vmem((k, T, F), BF16),
        x_sib=vmem((k, T, F), BF16),
        j_own=vmem((k, T, W), F32),
        j_send=vmem((o, k, T, W), BF16),
        j_recv=vmem((o, k, T, W), BF16),
        st_own=vmem((k, 1, LANES), F32),
        st_recv=vmem((o, k, 1, LANES), F32),
        qkv=vmem((k, T, W), BF16),
        r_all=vmem((k, T, LANES), F32),
        probs=vmem((k, H // HEAD_DIM * T, T), F32),
        mixed=vmem((k, T, H), BF16),
        mixed_sib=vmem((k, T, H), BF16),
        y_own=vmem((k, T, F), F32),
        y_send=vmem((o, k, T, F), BF16),
        y_recv=vmem((o, k, T, F), BF16),
        z_send=vmem((k, T, F), BF16),
        u_all=vmem((n, k, T, F), BF16),
        g_all=vmem((n, k, T, W), BF16),
        gs_all=vmem((n, k, 1, LANES), F32),
        gkv=vmem((k, T, W - H), BF16),
        normed=vmem((k, T, F), BF16),
        d_send=vmem((k, T, F), BF16),
        gain_acc=vmem((8, F), F32),
        gain_all=vmem((n, 1, F), F32),
        gj=vmem((F, J), F32),
        go=vmem((H, d.D), F32),
        w_l=dma((2 * d.chips + 4,)),
        w_s=dma((2 * d.chips + 1,)),
        w_r=dma((2 * d.chips + 1,)),
        b_s=dma((n - 1,)),
        b_r=dma((n - 1,)),
        n_s=dma((n - 1,)),
        n_r=dma((n - 1,)),
        d_s=dma((d.mb, n - 1)),
        g_s=dma((d.mb, n - 1)),
        o_s=dma((2 * n + 1,)),
    )
    for name in ("x_r", "u_r", "xs_s", "xs_r", "m_s", "m_r", "z_s", "dz_s"):
        scratch[name] = each
    for name in ("us_s", "us_r", "gs_s", "gs_r", "hs_s", "hs_r"):
        scratch[name] = each
    for name in ("j", "st", "y", "ux", "ur", "gx", "gr", "hx", "hr"):
        scratch[name + "_s"] = cross
        scratch[name + "_r"] = cross
    d.names = list(scratch)
    anywhere = pl.BlockSpec(memory_space=pl.ANY)
    inside = pl.BlockSpec(memory_space=pltpu.VMEM)
    return pl.pallas_call(
        functools.partial(step_kernel, d),
        out_shape=[
            jax.ShapeDtypeStruct((F, J), F32),
            jax.ShapeDtypeStruct((H, d.D), F32),
            jax.ShapeDtypeStruct((n, 1, F), F32),
        ],
        in_specs=[anywhere, anywhere, inside, inside, anywhere, anywhere],
        out_specs=[anywhere, anywhere, inside],
        scratch_shapes=list(scratch.values()),
        compiler_params=pltpu.CompilerParams(
            collective_id=0, has_side_effects=True, vmem_limit_bytes=58 << 20
        ),
    )(stream, ograd, bias, gain, wj, wo)


def body(stream_in, out_grad, mask_blocks, norm_gain, w_joined, w_out):
    n = lax.axis_size("dp")
    wj, wo = w_joined[0], w_out[0]
    mb, blocks, _ = mask_blocks.shape
    d = types.SimpleNamespace(
        n=n,
        S=lax.axis_size("section"),
        chips=n // CORES,
        mb=mb,
        k=mb * n,
        T=stream_in.shape[0] // mb,
        F=wj.shape[0],
        D=stream_in.shape[1],
    )
    real = wo.shape[0]
    d.H = -(-real // LANES) * LANES
    d.W = d.H + 2 * HEAD_DIM
    pad = d.H - real
    if pad:
        heads = wj[:, : n * real].reshape(d.F, n, real)
        heads = jnp.pad(heads, ((0, 0), (0, 0), (0, pad))).reshape(d.F, n * d.H)
        wj = jnp.concatenate([heads, wj[:, n * real :]], axis=1)
        wo = jnp.pad(wo, ((0, pad), (0, 0)))
    hits = mask_blocks[:, :, :, None] == jnp.arange(blocks, dtype=jnp.int32)
    bias = jnp.where(jnp.any(hits, axis=2), 0.0, -1e30).astype(F32)
    bias = jnp.repeat(bias, BLOCK_LEN, axis=2)
    bias = jnp.pad(bias, ((0, 0), (0, -blocks % 8), (0, LANES - bias.shape[2])))
    gj, go, gain = train_step(d, stream_in, out_grad, bias, norm_gain, wj, wo)
    if pad:
        heads = gj[:, : n * d.H].reshape(d.F, n, d.H)[:, :, :real].reshape(d.F, n * real)
        gj = jnp.concatenate([heads, gj[:, n * d.H :]], axis=1)
        go = go[:real]
    return gj[None], go[None], gain.reshape(1, -1)


def solution(mesh):
    return jax.shard_map(
        body,
        mesh=mesh,
        in_specs=(
            P(("groups", "dp"), None),
            P(("groups", "dp"), None),
            P(("groups", "dp"), None, None),
            P("section", None),
            P("section", "dp", None),
            P("section", "dp", None),
        ),
        out_specs=(
            P(("groups", "section"), "dp", None),
            P(("groups", "section"), "dp", None),
            P(("groups", "section"), None),
        ),
        check_vma=False,
    )
```

```python
import functools
import types

import jax
import jax.numpy as jnp
from jax import lax
from jax.experimental import pallas as pl
from jax.experimental.pallas import tpu as pltpu
from jax.sharding import PartitionSpec as P

HEAD_DIM = 64
BLOCK_LEN = 16
LANES = 128
CORES = 2
EPSILON = 1e-05
F32 = jnp.float32
BF16 = jnp.bfloat16
NN = (((1,), (0,)), ((), ()))
NT = (((1,), (1,)), ((), ()))
TN = (((0,), (0,)), ((), ()))

LAG = dict(FA=0, F1=1, F2=2, F3=3, BA=0, B1=0, B3=2)
ORDER = ("BA", "F1", "F3", "FA", "B3", "F2", "B1")
FIRST_BACK = 2
STAGE_GAP = 11


def dot(left, right, dims=NN):
    return lax.dot_general(left, right, dims, preferred_element_type=F32)


def step_kernel(d, stream, ograd, masks, gain, wj, wo, *rest):
    outs, scratch = rest[:6], rest[6:]
    normed_out, mixed_out, g_out, gkv_out, u_out, gain_out = outs
    s = types.SimpleNamespace(**dict(zip(d.names, scratch)))
    n, k, T, F, H, W, chips = d.n, d.k, d.T, d.F, d.H, d.W, d.chips
    me = lax.axis_index("dp")
    sec = lax.axis_index("section")
    last = d.S - 1
    chip, core = me // CORES, lax.rem(me, CORES)
    sib = me + 1 - 2 * core
    others = range(1, chips)

    def ahead(kk):
        return lax.rem(chip + kk, chips) * CORES

    def behind(kk):
        return lax.rem(chip + chips - kk, chips) * CORES

    def push(src, dst, send, recv, device):
        pltpu.make_async_remote_copy(
            src_ref=src,
            dst_ref=dst,
            send_sem=send,
            recv_sem=recv,
            device_id=device,
            device_id_type=pl.DeviceIdType.MESH,
        ).start()

    def done(ref, sem):
        pltpu.make_async_copy(ref, ref, sem).wait()

    def cols(index, width):
        return pl.ds(pl.multiple_of(index * width, LANES), width)

    to_sib = {"dp": sib}

    def column(kk):
        return pl.ds(0, H) if kk == 0 else pl.ds(W + (kk - 1) * H, H)

    def pieces(which):
        out = []
        for kk in range(chips):
            e = ahead(kk) + which
            out.append((wj, cols(e, H), s.wjf, column(kk)))
        out.append((wj, pl.ds(n * H, W - H), s.wjf, pl.ds(H, W - H)))
        for kk in range(chips):
            e = ahead(kk) + which
            out.append((wo, cols(e, F), s.wof, pl.ds(kk * F, F)))
        return out

    loads = []
    for i, (src, there, dst, here) in enumerate(pieces(core)):
        rows = src.shape[0]
        loads.append(
            pltpu.make_async_copy(
                src.at[:, there], dst.at[pl.ds(0, rows), here], s.w_l.at[i]
            )
        )
    loads.append(pltpu.make_async_copy(wj, s.wj_own, s.w_l.at[2 * chips + 1]))
    loads.append(pltpu.make_async_copy(wo, s.wo_own, s.w_l.at[2 * chips + 2]))
    for copy in loads:
        copy.start()

    bias = s.bias_all.at[me]
    block_of = lax.broadcasted_iota(jnp.int32, (1, LANES), 1) // BLOCK_LEN
    for m in range(d.mb):
        for q in range(masks.shape[1]):
            hit = block_of == masks[m, q, 0]
            for j in range(1, masks.shape[2]):
                hit = jnp.logical_or(hit, block_of == masks[m, q, j])
            s.bias_all[me, m, q : q + 1, :] = jnp.where(hit, 0.0, -1e30)

    barrier = pltpu.get_barrier_semaphore()

    def greet(device):
        pl.semaphore_signal(
            barrier, inc=1, device_id=device, device_id_type=pl.DeviceIdType.MESH
        )

    for shift in range(1, n):
        greet({"dp": lax.rem(me + shift, n)})

    @pl.when(sec > 0)
    def _():
        for kk in range(chips):
            greet({"section": sec - 1, "dp": ahead(kk) + core})

    @pl.when(sec < last)
    def _():
        for kk in range(chips):
            greet({"section": sec + 1, "dp": ahead(kk) + core})

    ends = (sec > 0).astype(jnp.int32) + (sec < last).astype(jnp.int32)
    pl.semaphore_wait(barrier, n - 1 + chips * ends)

    def local(src, dst, sem):
        pltpu.make_async_copy(src, dst, sem).start()

    @pl.when(sec == 0)
    def _():
        for i in range(d.mb):
            t = i * n + me
            rows = pl.ds(i * T, T)
            local(stream.at[rows, cols(me, F)], s.x_own.at[t], s.x_r.at[t])
            for shift in range(1, n):
                e = lax.rem(me + shift, n)
                push(
                    stream.at[rows, cols(e, F)],
                    s.x_own.at[t],
                    s.d_s.at[i, shift - 1],
                    s.x_r.at[t],
                    {"dp": e},
                )

    for i, (src, there, dst, here) in enumerate(pieces(1 - core)):
        rows = src.shape[0]
        push(
            src.at[:, there],
            dst.at[pl.ds(rows, rows), here],
            s.w_s.at[i],
            s.w_r.at[i],
            to_sib,
        )

    for shift in range(1, n):
        e = lax.rem(me + shift, n)
        push(bias, bias, s.b_s.at[shift - 1], s.b_r.at[shift - 1], {"dp": e})

    @pl.when(sec == last)
    def _():
        for i in range(d.mb):
            t = i * n + me
            rows = pl.ds(i * T, T)
            for shift in range(n):
                e = lax.rem(me + shift, n)
                for kk in range(chips):
                    f = lax.rem(e // CORES + chips - kk, chips) * CORES + lax.rem(e, CORES)
                    recv = s.u_r.at[t] if kk == 0 else s.ux_r.at[kk - 1, t]
                    there, here = ograd.at[rows, cols(f, F)], s.u_all.at[f, t]
                    if shift:
                        push(there, here, s.g_s.at[i, shift - 1, kk], recv, {"dp": e})
                    else:
                        local(there, here, recv)

    s.gain_acc[...] = jnp.zeros_like(s.gain_acc)
    for copy in loads:
        copy.wait()
    for i, (src, there, dst, here) in enumerate(pieces(core)):
        rows = src.shape[0]
        done(dst.at[pl.ds(rows, rows), here], s.w_r.at[i])
    for shift in range(1, n):
        done(s.bias_all.at[lax.rem(me + n - shift, n)], s.b_r.at[shift - 1])

    def eye():
        return lax.broadcasted_iota(jnp.int32, (T, LANES), 0) == lax.broadcasted_iota(
            jnp.int32, (T, LANES), 1
        )

    def to_row(column_values):
        return jnp.sum(jnp.where(eye(), column_values, 0.0), axis=0, keepdims=True)

    def to_column(row_values):
        return jnp.sum(
            jnp.where(eye(), jnp.broadcast_to(row_values, (T, LANES)), 0.0), axis=1, keepdims=True
        )

    def low_half(rows):
        return lax.broadcasted_iota(jnp.int32, (rows, LANES), 1) < HEAD_DIM

    def stack_heads(rows):
        low = low_half(T)
        out = []
        for pair in range(H // LANES):
            both = rows[:, pair * LANES : (pair + 1) * LANES]
            out += [jnp.where(low, both, 0.0), jnp.where(low, 0.0, both)]
        return jnp.concatenate(out, axis=0)

    def unstack_heads(rows):
        low = low_half(T)
        out = []
        for pair in range(H // LANES):
            first = rows[2 * pair * T : (2 * pair + 1) * T]
            second = rows[(2 * pair + 1) * T : (2 * pair + 2) * T]
            out.append(jnp.where(low, first, second))
        return jnp.concatenate(out, axis=1)

    def doubled(kv):
        low = low_half(T)
        turned = pltpu.roll(kv, HEAD_DIM, 1)
        return jnp.where(low, kv, turned).astype(BF16), jnp.where(low, turned, kv).astype(BF16)

    peers = [sib] + [ahead(kk) + c for kk in others for c in (core, 1 - core)]
    sources = [sib] + [behind(kk) + c for kk in others for c in (core, 1 - core)]
    g_own = gain[:, cols(me, F)]
    g_sib = gain[:, cols(sib, F)]

    def fa(t):
        @pl.when(sec == 0)
        def _():
            done(s.x_own.at[t], s.x_r.at[t])

        @pl.when(sec > 0)
        def _():
            done(s.x_near.at[t], s.x_r.at[t])
            total = s.x_near[t].astype(F32)
            for kk in others:
                at = (kk - 1, t)
                done(s.x_far.at[at], s.xf_r.at[at])
                total = total + s.x_far[at].astype(F32)
            s.x_own[t] = total.astype(BF16)

        push(s.x_own.at[t], s.x_sib.at[t], s.xs_s.at[t], s.xs_r.at[t], to_sib)

    def f1(t):
        own = s.x_own[t].astype(F32)
        done(s.x_sib.at[t], s.xs_r.at[t])
        beside = s.x_sib[t].astype(F32)
        squares = jnp.sum(own * own, axis=1, keepdims=True) + jnp.sum(
            beside * beside, axis=1, keepdims=True
        )
        part = dot((own * g_own).astype(BF16), s.wjf[:F]) + dot(
            (beside * g_sib).astype(BF16), s.wjf[F:]
        )
        s.j_own[t] = part[:, :W]
        s.st_own[t] = to_row(squares)
        for kk in others:
            s.j_send[kk - 1, t, :, :H] = part[:, W + (kk - 1) * H : W + kk * H].astype(BF16)
            s.j_send[kk - 1, t, :, H:] = part[:, H:W].astype(BF16)
        for kk in others:
            there = {"dp": ahead(kk) + core}
            at = (kk - 1, t)
            push(s.j_send.at[at], s.j_recv.at[at], s.j_s.at[at], s.j_r.at[at], there)
            push(s.st_own.at[t], s.st_recv.at[at], s.st_s.at[at], s.st_r.at[at], there)
        done(s.x_own.at[t], s.xs_s.at[t])

    def f2(t):
        total = s.j_own[t]
        squares = s.st_own[t]
        for kk in others:
            at = (kk - 1, t)
            done(s.j_recv.at[at], s.j_r.at[at])
            done(s.st_recv.at[at], s.st_r.at[at])
            total = total + s.j_recv[at].astype(F32)
            squares = squares + s.st_recv[at]
        inv_rms = lax.rsqrt(to_column(squares) / d.D + EPSILON)
        joined = (total * inv_rms).astype(BF16)
        s.qkv[t] = joined
        s.r_all[t] = jnp.broadcast_to(inv_rms, (T, LANES))
        wide = joined.astype(F32)
        queries = stack_heads(wide[:, :H]).astype(BF16)
        kk_rows, vv_rows = doubled(wide[:, H:])
        scores = dot(queries, kk_rows, NT) * HEAD_DIM ** (-0.5)
        blocks = s.bias_all[lax.rem(t, n), t // n]
        rows = [
            jnp.broadcast_to(blocks[b : b + 1, :T], (BLOCK_LEN, T)) for b in range(T // BLOCK_LEN)
        ]
        scores = scores + jnp.concatenate(rows * (H // HEAD_DIM), axis=0)
        exps = jnp.exp(scores - jnp.max(scores, axis=1, keepdims=True))
        probs = exps / jnp.sum(exps, axis=1, keepdims=True)
        s.probs[t] = probs
        s.mixed[t] = unstack_heads(dot(probs.astype(BF16), vv_rows)).astype(BF16)
        local(s.mixed.at[t], mixed_out.at[t], s.o_s.at[0, t])

        @pl.when(sec < last)
        def _():
            push(s.mixed.at[t], s.mixed_sib.at[t], s.m_s.at[t], s.m_r.at[t], to_sib)

        for kk in others:
            at = (kk - 1, t)
            done(s.j_send.at[at], s.j_s.at[at])
            done(s.st_own.at[t], s.st_s.at[at])

    def f3(t):
        @pl.when(sec < last)
        def _():
            done(s.mixed_sib.at[t], s.m_r.at[t])
            part = dot(s.mixed[t], s.wof[:H]) + dot(s.mixed_sib[t], s.wof[H:])
            for kk in others:
                at = (kk - 1, t)
                s.y_send[at] = part[:, kk * F : (kk + 1) * F].astype(BF16)
                push(
                    s.y_send.at[at],
                    s.x_far.at[at],
                    s.y_s.at[at],
                    s.xf_r.at[at],
                    {"section": sec + 1, "dp": ahead(kk) + core},
                )
            s.z_send[t] = (part[:, :F] + s.x_own[t].astype(F32)).astype(BF16)
            push(s.z_send.at[t], s.x_near.at[t], s.z_s.at[t], s.x_r.at[t], {"section": sec + 1})
            done(s.mixed.at[t], s.m_s.at[t])

    def ba(t):
        mine = s.u_all.at[me, t]
        done(mine, s.u_r.at[t])
        push(mine, mine, s.us_s.at[t], s.us_r.at[t], to_sib)
        for kk in others:
            at = (kk - 1, t)
            block = s.u_all.at[behind(kk) + core, t]
            done(block, s.ux_r.at[at])
            push(block, block, s.ur_s.at[at], s.ur_r.at[at], to_sib)

    def b1(t):
        done(s.u_all.at[sib, t], s.us_r.at[t])
        for kk in others:
            done(s.u_all.at[behind(kk) + 1 - core, t], s.ur_r.at[kk - 1, t])
        upstream = jnp.concatenate([s.u_all[e, t] for e in range(n)], axis=1)
        grad_mixed = dot(upstream, s.wo_own[...], NT).astype(BF16).astype(F32)
        grads = stack_heads(grad_mixed).astype(BF16)
        joined = s.qkv[t].astype(F32)
        queries = stack_heads(joined[:, :H]).astype(BF16)
        kk_rows, vv_rows = doubled(joined[:, H:])
        probs = s.probs[t]
        grad_probs = dot(grads, vv_rows, NT)
        inner = jnp.sum(probs * grad_probs, axis=1, keepdims=True)
        grad_scores = (probs * (grad_probs - inner) * HEAD_DIM ** (-0.5)).astype(BF16)
        grad_values = dot(probs.astype(BF16), grads, TN)
        grad_keys = dot(grad_scores, queries, TN)
        grad_queries = unstack_heads(dot(grad_scores, kk_rows))
        grad_kv = jnp.where(
            low_half(T),
            grad_keys + pltpu.roll(grad_keys, HEAD_DIM, 1),
            grad_values + pltpu.roll(grad_values, HEAD_DIM, 1),
        )
        message = jnp.concatenate([grad_queries, grad_kv], axis=1)
        s.g_all[me, t] = message.astype(BF16)
        s.gs_all[me, t] = to_row(jnp.sum(message * joined, axis=1, keepdims=True))
        mine, stat = s.g_all.at[me, t], s.gs_all.at[me, t]
        for shift, e in enumerate(peers):
            at = (shift, t)
            push(mine, mine, s.gx_s.at[at], s.gx_r.at[at], {"dp": e})
            push(stat, stat, s.hx_s.at[at], s.hx_r.at[at], {"dp": e})
        local(s.u_all.at[:, t], u_out.at[:, t], s.o_s.at[1, t])
        done(s.u_all.at[me, t], s.us_s.at[t])
        for kk in others:
            done(s.u_all.at[behind(kk) + core, t], s.ur_s.at[kk - 1, t])

    def b3(t):
        for shift, e in enumerate(sources):
            done(s.g_all.at[e, t], s.gx_r.at[shift, t])
            done(s.gs_all.at[e, t], s.hx_r.at[shift, t])
        blocks = [s.g_all[e, t] for e in range(n)]
        grad_kv = functools.reduce(lambda a, b: a + b, [b[:, H:].astype(F32) for b in blocks])
        grad_kv = grad_kv.astype(BF16)
        s.gkv[t] = grad_kv
        rows = jnp.concatenate([b[:, :H] for b in blocks] + [grad_kv], axis=1)
        grad_normed = dot(rows, s.wj_own[...], NT)
        stat = functools.reduce(lambda a, b: a + b, [s.gs_all[e, t] for e in range(n)])
        inv_rms = s.r_all[t][:, :1]
        wide = s.x_own[t].astype(F32)
        scaled = wide * inv_rms
        s.normed[t] = (scaled * g_own).astype(BF16)
        s.gain_acc[...] += jnp.sum((grad_normed * scaled).reshape(T // 8, 8, F), axis=0)

        @pl.when(sec > 0)
        def _():
            mean = to_column(stat) / d.D
            down = s.u_all[me, t].astype(F32) + inv_rms * (g_own * grad_normed - scaled * mean)
            s.d_send[t] = down.astype(BF16)
            block = s.u_all.at[me, t]
            for kk in others:
                push(
                    s.d_send.at[t],
                    block,
                    s.dx_s.at[kk - 1, t],
                    s.ux_r.at[kk - 1, t],
                    {"section": sec - 1, "dp": ahead(kk) + core},
                )
            push(s.d_send.at[t], block, s.dz_s.at[t], s.u_r.at[t], {"section": sec - 1})

        local(s.normed.at[t], normed_out.at[t], s.o_s.at[2, t])
        local(s.g_all.at[:, t], g_out.at[:, t], s.o_s.at[3, t])
        local(s.gkv.at[t], gkv_out.at[t], s.o_s.at[4, t])
        for shift in range(n - 1):
            done(s.g_all.at[me, t], s.gx_s.at[shift, t])
            done(s.gs_all.at[me, t], s.hx_s.at[shift, t])

    phases = dict(FA=fa, F1=f1, F2=f2, F3=f3, BA=ba, B1=b1, B3=b3)
    gap = jnp.minimum(FIRST_BACK + STAGE_GAP * (last - sec), k + LAG["F3"])

    def step(now, carry):
        for name in ORDER:
            t = now - LAG[name] - (gap if name[0] != "F" else 0)

            @pl.when(jnp.logical_and(t >= 0, t < k))
            def _(name=name, t=t):
                phases[name](t)

        return carry

    lax.fori_loop(0, k + gap + LAG["B3"], step, 0)

    s.gain_all[me] = jnp.sum(s.gain_acc[...], axis=0, keepdims=True)
    for shift in range(1, n):
        push(
            s.gain_all.at[me],
            s.gain_all.at[me],
            s.n_s.at[shift - 1],
            s.n_r.at[shift - 1],
            {"dp": lax.rem(me + shift, n)},
        )
    for shift in range(1, n):
        done(s.gain_all.at[lax.rem(me + n - shift, n)], s.n_r.at[shift - 1])
        done(s.gain_all.at[me], s.n_s.at[shift - 1])
    gain_out[...] = s.gain_all[...]

    @pl.when(sec == 0)
    def _():
        for i in range(d.mb):
            for shift in range(n - 1):
                done(stream.at[pl.ds(i * T, T), pl.ds(0, F)], s.d_s.at[i, shift])

    @pl.when(sec == last)
    def _():
        for i in range(d.mb):
            for shift in range(n - 1):
                for kk in range(chips):
                    done(ograd.at[pl.ds(i * T, T), pl.ds(0, F)], s.g_s.at[i, shift, kk])

    for i, (src, there, dst, here) in enumerate(pieces(1 - core)):
        done(src.at[:, there], s.w_s.at[i])
    for shift in range(1, n):
        done(bias, s.b_s.at[shift - 1])

    def settle(t, carry):
        @pl.when(sec < last)
        def _():
            done(s.z_send.at[t], s.z_s.at[t])
            for kk in others:
                done(s.y_send.at[kk - 1, t], s.y_s.at[kk - 1, t])

        @pl.when(sec > 0)
        def _():
            done(s.d_send.at[t], s.dz_s.at[t])
            for kk in others:
                done(s.d_send.at[t], s.dx_s.at[kk - 1, t])

        done(s.mixed.at[t], s.o_s.at[0, t])
        done(s.u_all.at[:, t], s.o_s.at[1, t])
        done(s.normed.at[t], s.o_s.at[2, t])
        done(s.g_all.at[:, t], s.o_s.at[3, t])
        done(s.gkv.at[t], s.o_s.at[4, t])
        return carry

    lax.fori_loop(0, k, settle, 0)


def weights_kernel(d, normed_in, mixed_in, g_in, gkv_in, u_in, gain_in, *rest):
    gj_out, go_out, gain_out, normed, mixed, g, gkv, u, gj, go, in_sems, out_sems = rest
    n, F, H = d.n, d.F, d.H
    pairs = [(normed_in, normed), (mixed_in, mixed), (gkv_in, gkv)]
    for e in range(n):
        pairs += [(g_in.at[e], g.at[e]), (u_in.at[e], u.at[e])]
    loads = [pltpu.make_async_copy(a, b, in_sems.at[i]) for i, (a, b) in enumerate(pairs)]
    for i in [0, 3, 1, 4] + list(range(5, len(pairs))) + [2]:
        loads[i].start()
    stores = []

    def store(block, out, start, width):
        here = (slice(None), pl.ds(start, width))
        copy = pltpu.make_async_copy(block.at[here], out.at[here], out_sems.at[len(stores)])
        copy.start()
        stores.append(copy)

    gain_out[...] = jnp.concatenate([gain_in[e] for e in range(n)], axis=1)
    for e in range(n):
        if e == 0:
            loads[0].wait()
        loads[3 + 2 * e].wait()
        gj[:, e * H : (e + 1) * H] = dot(normed[...], g[e, :, :H], TN)
        store(gj, gj_out, e * H, H)
        if e == 0:
            loads[1].wait()
        loads[4 + 2 * e].wait()
        go[:, e * F : (e + 1) * F] = dot(mixed[...], u[e], TN)
        store(go, go_out, e * F, F)
    loads[2].wait()
    gj[:, n * H :] = dot(normed[...], gkv[...], TN)
    store(gj, gj_out, n * H, d.W - H)
    for copy in stores:
        copy.wait()


def train_step(d, stream, ograd, masks, gain, wj, wo):
    n, k, T, F, H, W = d.n, d.k, d.T, d.F, d.H, d.W
    o = d.chips - 1
    J = n * H + W - H
    vmem, dma = pltpu.VMEM, pltpu.SemaphoreType.DMA
    each, cross = dma((k,)), dma((o, k))
    scratch = dict(
        wjf=vmem((2 * F, W + o * H), BF16),
        wof=vmem((2 * H, d.chips * F), BF16),
        wj_own=vmem((F, J), BF16),
        wo_own=vmem((H, d.D), BF16),
        bias_all=vmem((n, d.mb, -(-masks.shape[1] // 8) * 8, LANES), F32),
        x_own=vmem((k, T, F), BF16),
        x_sib=vmem((k, T, F), BF16),
        j_own=vmem((k, T, W), F32),
        j_send=vmem((o, k, T, W), BF16),
        j_recv=vmem((o, k, T, W), BF16),
        st_own=vmem((k, 1, LANES), F32),
        st_recv=vmem((o, k, 1, LANES), F32),
        qkv=vmem((k, T, W), BF16),
        r_all=vmem((k, T, LANES), F32),
        probs=vmem((k, H // HEAD_DIM * T, T), F32),
        mixed=vmem((k, T, H), BF16),
        mixed_sib=vmem((k, T, H), BF16),
        x_near=vmem((k, T, F), BF16),
        x_far=vmem((o, k, T, F), BF16),
        y_send=vmem((o, k, T, F), BF16),
        z_send=vmem((k, T, F), BF16),
        u_all=vmem((n, k, T, F), BF16),
        g_all=vmem((n, k, T, W), BF16),
        gs_all=vmem((n, k, 1, LANES), F32),
        gkv=vmem((k, T, W - H), BF16),
        normed=vmem((k, T, F), BF16),
        d_send=vmem((k, T, F), BF16),
        gain_acc=vmem((8, F), F32),
        gain_all=vmem((n, 1, F), F32),
        w_l=dma((2 * d.chips + 3,)),
        w_s=dma((2 * d.chips + 1,)),
        w_r=dma((2 * d.chips + 1,)),
        b_s=dma((n - 1,)),
        b_r=dma((n - 1,)),
        n_s=dma((n - 1,)),
        n_r=dma((n - 1,)),
        d_s=dma((d.mb, n - 1)),
        g_s=dma((d.mb, n - 1, d.chips)),
        o_s=dma((5, k)),
    )
    for name in ("x_r", "u_r", "xs_s", "xs_r", "m_s", "m_r", "z_s", "dz_s"):
        scratch[name] = each
    for name in ("us_s", "us_r"):
        scratch[name] = each
    for name in ("j_s", "j_r", "st_s", "st_r", "y_s", "xf_r", "ux_r", "ur_s", "ur_r", "dx_s"):
        scratch[name] = cross
    for name in ("gx_s", "gx_r", "hx_s", "hx_r"):
        scratch[name] = dma((n - 1, k))
    d.names = list(scratch)
    anywhere = pl.BlockSpec(memory_space=pl.ANY)
    inside = pl.BlockSpec(memory_space=pltpu.VMEM)
    rows = k * T
    kept = [(k, T, F), (k, T, H), (n, k, T, W), (k, T, W - H), (n, k, T, F)]
    *blocks, gain_all = pl.pallas_call(
        functools.partial(step_kernel, d),
        out_shape=[jax.ShapeDtypeStruct(shape, BF16) for shape in kept]
        + [jax.ShapeDtypeStruct((n, 1, F), F32)],
        in_specs=[anywhere, anywhere, pl.BlockSpec(memory_space=pltpu.SMEM), inside]
        + [anywhere] * 2,
        out_specs=[anywhere] * 5 + [inside],
        scratch_shapes=list(scratch.values()),
        compiler_params=pltpu.CompilerParams(
            collective_id=0, has_side_effects=True, vmem_limit_bytes=58 << 20
        ),
    )(stream, ograd, masks, gain, wj, wo)
    flat = [(rows, F), (rows, H), (n, rows, W), (rows, W - H), (n, rows, F)]
    return pl.pallas_call(
        functools.partial(weights_kernel, d),
        out_shape=[
            jax.ShapeDtypeStruct((F, J), F32),
            jax.ShapeDtypeStruct((H, d.D), F32),
            jax.ShapeDtypeStruct((1, n * F), F32),
        ],
        in_specs=[anywhere] * 5 + [inside],
        out_specs=[anywhere] * 2 + [inside],
        scratch_shapes=[vmem(shape, BF16) for shape in flat]
        + [vmem((F, J), F32), vmem((H, d.D), F32), dma((2 * n + 3,)), dma((2 * n + 1,))],
        compiler_params=pltpu.CompilerParams(vmem_limit_bytes=48 << 20),
    )(*[block.reshape(shape) for block, shape in zip(blocks, flat)], gain_all)


def body(stream_in, out_grad, mask_blocks, norm_gain, w_joined, w_out):
    n = lax.axis_size("dp")
    wj, wo = w_joined[0], w_out[0]
    mb = mask_blocks.shape[0]
    d = types.SimpleNamespace(
        n=n,
        S=lax.axis_size("section"),
        chips=n // CORES,
        mb=mb,
        k=mb * n,
        T=stream_in.shape[0] // mb,
        F=wj.shape[0],
        D=stream_in.shape[1],
    )
    real = wo.shape[0]
    d.H = -(-real // LANES) * LANES
    d.W = d.H + 2 * HEAD_DIM
    pad = d.H - real
    if pad:
        heads = wj[:, : n * real].reshape(d.F, n, real)
        heads = jnp.pad(heads, ((0, 0), (0, 0), (0, pad))).reshape(d.F, n * d.H)
        wj = jnp.concatenate([heads, wj[:, n * real :]], axis=1)
        wo = jnp.pad(wo, ((0, pad), (0, 0)))
    gj, go, gain = train_step(d, stream_in, out_grad, mask_blocks, norm_gain, wj, wo)
    if pad:
        heads = gj[:, : n * d.H].reshape(d.F, n, d.H)[:, :, :real].reshape(d.F, n * real)
        gj = jnp.concatenate([heads, gj[:, n * d.H :]], axis=1)
        go = go[:real]
    return gj[None], go[None], gain


def solution(mesh):
    return jax.shard_map(
        body,
        mesh=mesh,
        in_specs=(
            P(("groups", "dp"), None),
            P(("groups", "dp"), None),
            P(("groups", "dp"), None, None),
            P("section", None),
            P("section", "dp", None),
            P("section", "dp", None),
        ),
        out_specs=(
            P(("groups", "section"), "dp", None),
            P(("groups", "section"), "dp", None),
            P(("groups", "section"), None),
        ),
        check_vma=False,
    )
```

```python
import functools
import types

import jax
import jax.numpy as jnp
from jax import lax
from jax.experimental import pallas as pl
from jax.experimental.pallas import tpu as pltpu
from jax.sharding import PartitionSpec as P

HEAD_DIM = 64
BLOCK_LEN = 16
LANES = 128
CORES = 2
EPSILON = 1e-05
F32 = jnp.float32
BF16 = jnp.bfloat16
NN = (((1,), (0,)), ((), ()))
NT = (((1,), (1,)), ((), ()))
TN = (((0,), (0,)), ((), ()))

LAG = dict(FA=0, F1=1, F2=2, F3=3, F4=4, BA=0, BR=1, BM=1, B1=2, GR=3, B3=3)
ORDER = ("BA", "F4", "F1", "F3", "BR", "GR", "BM", "FA", "B3", "F2", "B1")
FIRST_BACK = 0
STAGE_GAP = 11


def dot(left, right, dims=NN):
    return lax.dot_general(left, right, dims, preferred_element_type=F32)


def step_kernel(d, stream, ograd, masks, gain, wj, wo, *rest):
    outs, scratch = rest[:6], rest[6:]
    normed_out, mixed_out, g_out, gkv_out, u_out, gain_out = outs
    s = types.SimpleNamespace(**dict(zip(d.names, scratch)))
    n, k, T, F, H, W, chips = d.n, d.k, d.T, d.F, d.H, d.W, d.chips
    me = lax.axis_index("dp")
    sec = lax.axis_index("section")
    last = d.S - 1
    chip, core = me // CORES, lax.rem(me, CORES)
    sib = me + 1 - 2 * core
    others = range(1, chips)

    def ahead(kk):
        return lax.rem(chip + kk, chips) * CORES

    def behind(kk):
        return lax.rem(chip + chips - kk, chips) * CORES

    def push(src, dst, send, recv, device):
        pltpu.make_async_remote_copy(
            src_ref=src,
            dst_ref=dst,
            send_sem=send,
            recv_sem=recv,
            device_id=device,
            device_id_type=pl.DeviceIdType.MESH,
        ).start()

    def done(ref, sem):
        pltpu.make_async_copy(ref, ref, sem).wait()

    def cols(index, width):
        return pl.ds(pl.multiple_of(index * width, LANES), width)

    to_sib = {"dp": sib}

    def column(kk):
        return pl.ds(0, H) if kk == 0 else pl.ds(W + (kk - 1) * H, H)

    def pieces(which):
        out = []
        for kk in range(chips):
            e = ahead(kk) + which
            out.append((wj, cols(e, H), s.wjf, column(kk)))
        out.append((wj, pl.ds(n * H, W - H), s.wjf, pl.ds(H, W - H)))
        for kk in range(chips):
            e = ahead(kk) + which
            out.append((wo, cols(e, F), s.wof, pl.ds(kk * F, F)))
        return out

    loads = []
    for i, (src, there, dst, here) in enumerate(pieces(core)):
        rows = src.shape[0]
        loads.append(
            pltpu.make_async_copy(
                src.at[:, there], dst.at[pl.ds(0, rows), here], s.w_l.at[i]
            )
        )
    loads.append(pltpu.make_async_copy(wj, s.wj_own, s.w_l.at[2 * chips + 1]))
    loads.append(pltpu.make_async_copy(wo, s.wo_own, s.w_l.at[2 * chips + 2]))
    for copy in loads:
        copy.start()

    bias = s.bias_all.at[me]
    block_of = lax.broadcasted_iota(jnp.int32, (1, LANES), 1) // BLOCK_LEN
    for m in range(d.mb):
        for q in range(masks.shape[1]):
            hit = block_of == masks[m, q, 0]
            for j in range(1, masks.shape[2]):
                hit = jnp.logical_or(hit, block_of == masks[m, q, j])
            s.bias_all[me, m, q : q + 1, :] = jnp.where(hit, 0.0, -1e30)

    barrier = pltpu.get_barrier_semaphore()

    def greet(device):
        pl.semaphore_signal(
            barrier, inc=1, device_id=device, device_id_type=pl.DeviceIdType.MESH
        )

    for shift in range(1, n):
        greet({"dp": lax.rem(me + shift, n)})

    @pl.when(sec > 0)
    def _():
        greet({"section": sec - 1})

    @pl.when(sec < last)
    def _():
        greet({"section": sec + 1})

    ends = (sec > 0).astype(jnp.int32) + (sec < last).astype(jnp.int32)
    pl.semaphore_wait(barrier, n - 1 + ends)

    def local(src, dst, sem):
        pltpu.make_async_copy(src, dst, sem).start()

    @pl.when(sec == 0)
    def _():
        for i in range(d.mb):
            t = i * n + me
            rows = pl.ds(i * T, T)
            local(stream.at[rows, cols(me, F)], s.x_own.at[t], s.x_r.at[t])
            for shift in range(1, n):
                e = lax.rem(me + shift, n)
                push(
                    stream.at[rows, cols(e, F)],
                    s.x_own.at[t],
                    s.d_s.at[i, shift - 1],
                    s.x_r.at[t],
                    {"dp": e},
                )

    for i, (src, there, dst, here) in enumerate(pieces(1 - core)):
        rows = src.shape[0]
        push(
            src.at[:, there],
            dst.at[pl.ds(rows, rows), here],
            s.w_s.at[i],
            s.w_r.at[i],
            to_sib,
        )

    for shift in range(1, n):
        e = lax.rem(me + shift, n)
        push(bias, bias, s.b_s.at[shift - 1], s.b_r.at[shift - 1], {"dp": e})

    @pl.when(sec == last)
    def _():
        for i in range(d.mb):
            t = i * n + me
            rows = pl.ds(i * T, T)
            local(ograd.at[rows, cols(me, F)], s.u_all.at[me, t], s.u_r.at[t])
            for shift in range(1, n):
                e = lax.rem(me + shift, n)
                push(
                    ograd.at[rows, cols(e, F)],
                    s.u_all.at[e, t],
                    s.g_s.at[i, shift - 1],
                    s.u_r.at[t],
                    {"dp": e},
                )

    s.gain_acc[...] = jnp.zeros_like(s.gain_acc)
    for copy in loads:
        copy.wait()
    for i, (src, there, dst, here) in enumerate(pieces(core)):
        rows = src.shape[0]
        done(dst.at[pl.ds(rows, rows), here], s.w_r.at[i])
    for shift in range(1, n):
        done(s.bias_all.at[lax.rem(me + n - shift, n)], s.b_r.at[shift - 1])

    def eye():
        return lax.broadcasted_iota(jnp.int32, (T, LANES), 0) == lax.broadcasted_iota(
            jnp.int32, (T, LANES), 1
        )

    def to_row(column_values):
        return jnp.sum(jnp.where(eye(), column_values, 0.0), axis=0, keepdims=True)

    def to_column(row_values):
        return jnp.sum(
            jnp.where(eye(), jnp.broadcast_to(row_values, (T, LANES)), 0.0), axis=1, keepdims=True
        )

    def low_half(rows):
        return lax.broadcasted_iota(jnp.int32, (rows, LANES), 1) < HEAD_DIM

    def stack_heads(rows):
        low = low_half(T)
        out = []
        for pair in range(H // LANES):
            both = rows[:, pair * LANES : (pair + 1) * LANES]
            out += [jnp.where(low, both, 0.0), jnp.where(low, 0.0, both)]
        return jnp.concatenate(out, axis=0)

    def unstack_heads(rows):
        low = low_half(T)
        out = []
        for pair in range(H // LANES):
            first = rows[2 * pair * T : (2 * pair + 1) * T]
            second = rows[(2 * pair + 1) * T : (2 * pair + 2) * T]
            out.append(jnp.where(low, first, second))
        return jnp.concatenate(out, axis=1)

    def doubled(kv):
        low = low_half(T)
        turned = pltpu.roll(kv, HEAD_DIM, 1)
        return jnp.where(low, kv, turned).astype(BF16), jnp.where(low, turned, kv).astype(BF16)

    peers = [sib] + [ahead(kk) + c for kk in others for c in (core, 1 - core)]
    sources = [sib] + [behind(kk) + c for kk in others for c in (core, 1 - core)]
    g_own = gain[:, cols(me, F)]
    g_sib = gain[:, cols(sib, F)]

    def fa(t):
        done(s.x_own.at[t], s.x_r.at[t])
        push(s.x_own.at[t], s.x_sib.at[t], s.xs_s.at[t], s.xs_r.at[t], to_sib)

    def f1(t):
        own = s.x_own[t].astype(F32)
        done(s.x_sib.at[t], s.xs_r.at[t])
        beside = s.x_sib[t].astype(F32)
        squares = jnp.sum(own * own, axis=1, keepdims=True) + jnp.sum(
            beside * beside, axis=1, keepdims=True
        )
        part = dot((own * g_own).astype(BF16), s.wjf[:F]) + dot(
            (beside * g_sib).astype(BF16), s.wjf[F:]
        )
        s.j_own[t] = part[:, :W]
        s.st_own[t] = to_row(squares)
        for kk in others:
            s.j_send[kk - 1, t, :, :H] = part[:, W + (kk - 1) * H : W + kk * H].astype(BF16)
            s.j_send[kk - 1, t, :, H:] = part[:, H:W].astype(BF16)
        for kk in others:
            there = {"dp": ahead(kk) + core}
            at = (kk - 1, t)
            push(s.j_send.at[at], s.j_recv.at[at], s.j_s.at[at], s.j_r.at[at], there)
            push(s.st_own.at[t], s.st_recv.at[at], s.st_s.at[at], s.st_r.at[at], there)
        done(s.x_own.at[t], s.xs_s.at[t])

    def f2(t):
        total = s.j_own[t]
        squares = s.st_own[t]
        for kk in others:
            at = (kk - 1, t)
            done(s.j_recv.at[at], s.j_r.at[at])
            done(s.st_recv.at[at], s.st_r.at[at])
            total = total + s.j_recv[at].astype(F32)
            squares = squares + s.st_recv[at]
        inv_rms = lax.rsqrt(to_column(squares) / d.D + EPSILON)
        joined = (total * inv_rms).astype(BF16)
        s.qkv[t] = joined
        s.r_all[t] = jnp.broadcast_to(inv_rms, (T, LANES))
        wide = joined.astype(F32)
        queries = stack_heads(wide[:, :H]).astype(BF16)
        kk_rows, vv_rows = doubled(wide[:, H:])
        scores = dot(queries, kk_rows, NT) * HEAD_DIM ** (-0.5)
        blocks = s.bias_all[lax.rem(t, n), t // n]
        rows = [
            jnp.broadcast_to(blocks[b : b + 1, :T], (BLOCK_LEN, T)) for b in range(T // BLOCK_LEN)
        ]
        scores = scores + jnp.concatenate(rows * (H // HEAD_DIM), axis=0)
        exps = jnp.exp(scores - jnp.max(scores, axis=1, keepdims=True))
        probs = exps / jnp.sum(exps, axis=1, keepdims=True)
        s.probs[t] = probs
        s.mixed[t] = unstack_heads(dot(probs.astype(BF16), vv_rows)).astype(BF16)
        local(s.mixed.at[t], mixed_out.at[t], s.o_s.at[0, t])

        @pl.when(sec < last)
        def _():
            push(s.mixed.at[t], s.mixed_sib.at[t], s.m_s.at[t], s.m_r.at[t], to_sib)

        for kk in others:
            at = (kk - 1, t)
            done(s.j_send.at[at], s.j_s.at[at])
            done(s.st_own.at[t], s.st_s.at[at])

    def f3(t):
        @pl.when(sec < last)
        def _():
            done(s.mixed_sib.at[t], s.m_r.at[t])
            part = dot(s.mixed[t], s.wof[:H]) + dot(s.mixed_sib[t], s.wof[H:])
            for kk in others:
                at = (kk - 1, t)
                s.y_send[at] = part[:, kk * F : (kk + 1) * F].astype(BF16)
                push(
                    s.y_send.at[at],
                    s.y_recv.at[at],
                    s.y_s.at[at],
                    s.y_r.at[at],
                    {"dp": ahead(kk) + core},
                )
            s.y_own[t] = part[:, :F] + s.x_own[t].astype(F32)
            done(s.mixed.at[t], s.m_s.at[t])

    def f4(t):
        @pl.when(sec < last)
        def _():
            total = s.y_own[t]
            for kk in others:
                at = (kk - 1, t)
                done(s.y_recv.at[at], s.y_r.at[at])
                total = total + s.y_recv[at].astype(F32)
            s.z_send[t] = total.astype(BF16)
            push(s.z_send.at[t], s.x_own.at[t], s.z_s.at[t], s.x_r.at[t], {"section": sec + 1})
            for kk in others:
                done(s.y_send.at[kk - 1, t], s.y_s.at[kk - 1, t])

    def ba(t):
        mine = s.u_all.at[me, t]
        done(mine, s.u_r.at[t])
        for kk in others:
            at = (kk - 1, t)
            push(mine, mine, s.ux_s.at[at], s.ux_r.at[at], {"dp": ahead(kk) + core})
        push(mine, mine, s.us_s.at[t], s.us_r.at[t], to_sib)

    def br(t):
        for kk in others:
            at = (kk - 1, t)
            block = s.u_all.at[behind(kk) + core, t]
            done(block, s.ux_r.at[at])
            push(block, block, s.ur_s.at[at], s.ur_r.at[at], to_sib)

    def bm(t):
        done(s.u_all.at[sib, t], s.us_r.at[t])
        for kk in others:
            done(s.u_all.at[behind(kk) + 1 - core, t], s.ur_r.at[kk - 1, t])
        upstream = jnp.concatenate([s.u_all[e, t] for e in range(n)], axis=1)
        s.gm[t] = dot(upstream, s.wo_own[...], NT).astype(BF16)
        local(s.u_all.at[:, t], u_out.at[:, t], s.o_s.at[1, t])
        done(s.u_all.at[me, t], s.us_s.at[t])
        for kk in others:
            done(s.u_all.at[me, t], s.ux_s.at[kk - 1, t])
            done(s.u_all.at[behind(kk) + core, t], s.ur_s.at[kk - 1, t])

    def b1(t):
        grads = stack_heads(s.gm[t].astype(F32)).astype(BF16)
        joined = s.qkv[t].astype(F32)
        queries = stack_heads(joined[:, :H]).astype(BF16)
        kk_rows, vv_rows = doubled(joined[:, H:])
        probs = s.probs[t]
        grad_probs = dot(grads, vv_rows, NT)
        inner = jnp.sum(probs * grad_probs, axis=1, keepdims=True)
        grad_scores = (probs * (grad_probs - inner) * HEAD_DIM ** (-0.5)).astype(BF16)
        grad_values = dot(probs.astype(BF16), grads, TN)
        grad_keys = dot(grad_scores, queries, TN)
        grad_queries = unstack_heads(dot(grad_scores, kk_rows))
        grad_kv = jnp.where(
            low_half(T),
            grad_keys + pltpu.roll(grad_keys, HEAD_DIM, 1),
            grad_values + pltpu.roll(grad_values, HEAD_DIM, 1),
        )
        message = jnp.concatenate([grad_queries, grad_kv], axis=1)
        s.g_all[me, t] = message.astype(BF16)
        s.gs_all[me, t] = to_row(jnp.sum(message * joined, axis=1, keepdims=True))
        mine, stat = s.g_all.at[me, t], s.gs_all.at[me, t]
        for kk in others:
            at = (kk - 1, t)
            push(mine, mine, s.gx_s.at[at], s.gx_r.at[at], {"dp": ahead(kk) + core})
        push(mine, mine, s.gs_s.at[t], s.gs_r.at[t], to_sib)
        for shift, e in enumerate(peers):
            at = (shift, t)
            push(stat, stat, s.hx_s.at[at], s.hx_r.at[at], {"dp": e})

    def gr(t):
        for kk in others:
            at = (kk - 1, t)
            block = s.g_all.at[behind(kk) + core, t]
            done(block, s.gx_r.at[at])
            push(block, block, s.gr_s.at[at], s.gr_r.at[at], to_sib)

    def b3(t):
        done(s.g_all.at[sib, t], s.gs_r.at[t])
        for kk in others:
            done(s.g_all.at[behind(kk) + 1 - core, t], s.gr_r.at[kk - 1, t])
        for shift, e in enumerate(sources):
            done(s.gs_all.at[e, t], s.hx_r.at[shift, t])
        blocks = [s.g_all[e, t] for e in range(n)]
        grad_kv = functools.reduce(lambda a, b: a + b, [b[:, H:].astype(F32) for b in blocks])
        grad_kv = grad_kv.astype(BF16)
        s.gkv[t] = grad_kv
        rows = jnp.concatenate([b[:, :H] for b in blocks] + [grad_kv], axis=1)
        grad_normed = dot(rows, s.wj_own[...], NT)
        stat = functools.reduce(lambda a, b: a + b, [s.gs_all[e, t] for e in range(n)])
        inv_rms = s.r_all[t][:, :1]
        wide = s.x_own[t].astype(F32)
        scaled = wide * inv_rms
        s.normed[t] = (scaled * g_own).astype(BF16)
        s.gain_acc[...] += jnp.sum((grad_normed * scaled).reshape(T // 8, 8, F), axis=0)

        @pl.when(sec > 0)
        def _():
            mean = to_column(stat) / d.D
            down = s.u_all[me, t].astype(F32) + inv_rms * (g_own * grad_normed - scaled * mean)
            s.d_send[t] = down.astype(BF16)
            push(
                s.d_send.at[t], s.u_all.at[me, t], s.dz_s.at[t], s.u_r.at[t], {"section": sec - 1}
            )

        local(s.normed.at[t], normed_out.at[t], s.o_s.at[2, t])
        local(s.g_all.at[:, t], g_out.at[:, t], s.o_s.at[3, t])
        local(s.gkv.at[t], gkv_out.at[t], s.o_s.at[4, t])
        done(s.g_all.at[me, t], s.gs_s.at[t])
        for kk in others:
            done(s.g_all.at[me, t], s.gx_s.at[kk - 1, t])
            done(s.g_all.at[behind(kk) + core, t], s.gr_s.at[kk - 1, t])
        for shift in range(n - 1):
            done(s.gs_all.at[me, t], s.hx_s.at[shift, t])

    @pl.when(sec == last)
    def _():
        for phase in (ba, br, bm):
            lax.fori_loop(0, k, lambda t, c, phase=phase: (phase(t), c)[1], 0)

    phases = dict(FA=fa, F1=f1, F2=f2, F3=f3, F4=f4, BA=ba, BR=br, BM=bm, B1=b1, GR=gr, B3=b3)
    gap = jnp.minimum(FIRST_BACK + STAGE_GAP * (last - sec), k + LAG["F4"])

    def step(now, carry):
        for name in ORDER:
            t = now - LAG[name] - (gap if name[0] != "F" else 0)
            run = jnp.logical_and(t >= 0, t < k)
            if name in ("BA", "BR", "BM"):
                run = jnp.logical_and(run, sec < last)

            @pl.when(run)
            def _(name=name, t=t):
                phases[name](t)

        return carry

    lax.fori_loop(0, k + jnp.maximum(gap + LAG["B3"], LAG["F4"]), step, 0)

    s.gain_all[me] = jnp.sum(s.gain_acc[...], axis=0, keepdims=True)
    for shift in range(1, n):
        push(
            s.gain_all.at[me],
            s.gain_all.at[me],
            s.n_s.at[shift - 1],
            s.n_r.at[shift - 1],
            {"dp": lax.rem(me + shift, n)},
        )
    for shift in range(1, n):
        done(s.gain_all.at[lax.rem(me + n - shift, n)], s.n_r.at[shift - 1])
        done(s.gain_all.at[me], s.n_s.at[shift - 1])
    gain_out[...] = s.gain_all[...]

    @pl.when(sec == 0)
    def _():
        for i in range(d.mb):
            for shift in range(n - 1):
                done(stream.at[pl.ds(i * T, T), pl.ds(0, F)], s.d_s.at[i, shift])

    @pl.when(sec == last)
    def _():
        for i in range(d.mb):
            for shift in range(n - 1):
                done(ograd.at[pl.ds(i * T, T), pl.ds(0, F)], s.g_s.at[i, shift])

    for i, (src, there, dst, here) in enumerate(pieces(1 - core)):
        done(src.at[:, there], s.w_s.at[i])
    for shift in range(1, n):
        done(bias, s.b_s.at[shift - 1])

    def settle(t, carry):
        @pl.when(sec < last)
        def _():
            done(s.z_send.at[t], s.z_s.at[t])

        @pl.when(sec > 0)
        def _():
            done(s.d_send.at[t], s.dz_s.at[t])

        done(s.mixed.at[t], s.o_s.at[0, t])
        done(s.u_all.at[:, t], s.o_s.at[1, t])
        done(s.normed.at[t], s.o_s.at[2, t])
        done(s.g_all.at[:, t], s.o_s.at[3, t])
        done(s.gkv.at[t], s.o_s.at[4, t])
        return carry

    lax.fori_loop(0, k, settle, 0)


def weights_kernel(d, normed_in, mixed_in, g_in, gkv_in, u_in, gain_in, *rest):
    gj_out, go_out, gain_out, normed, mixed, g, gkv, u, gj, go, in_sems, out_sems = rest
    n, F, H = d.n, d.F, d.H
    pairs = [(normed_in, normed), (mixed_in, mixed), (gkv_in, gkv)]
    for e in range(n):
        pairs += [(g_in.at[e], g.at[e]), (u_in.at[e], u.at[e])]
    loads = [pltpu.make_async_copy(a, b, in_sems.at[i]) for i, (a, b) in enumerate(pairs)]
    for i in [0, 3, 1, 4] + list(range(5, len(pairs))) + [2]:
        loads[i].start()
    stores = []

    def store(block, out, start, width):
        here = (slice(None), pl.ds(start, width))
        copy = pltpu.make_async_copy(block.at[here], out.at[here], out_sems.at[len(stores)])
        copy.start()
        stores.append(copy)

    gain_out[...] = jnp.concatenate([gain_in[e] for e in range(n)], axis=1)
    for e in range(n):
        if e == 0:
            loads[0].wait()
        loads[3 + 2 * e].wait()
        gj[:, e * H : (e + 1) * H] = dot(normed[...], g[e, :, :H], TN)
        store(gj, gj_out, e * H, H)
        if e == 0:
            loads[1].wait()
        loads[4 + 2 * e].wait()
        go[:, e * F : (e + 1) * F] = dot(mixed[...], u[e], TN)
        store(go, go_out, e * F, F)
    loads[2].wait()
    gj[:, n * H :] = dot(normed[...], gkv[...], TN)
    store(gj, gj_out, n * H, d.W - H)
    for copy in stores:
        copy.wait()


def train_step(d, stream, ograd, masks, gain, wj, wo):
    n, k, T, F, H, W = d.n, d.k, d.T, d.F, d.H, d.W
    o = d.chips - 1
    J = n * H + W - H
    vmem, dma = pltpu.VMEM, pltpu.SemaphoreType.DMA
    each, cross = dma((k,)), dma((o, k))
    scratch = dict(
        wjf=vmem((2 * F, W + o * H), BF16),
        wof=vmem((2 * H, d.chips * F), BF16),
        wj_own=vmem((F, J), BF16),
        wo_own=vmem((H, d.D), BF16),
        bias_all=vmem((n, d.mb, -(-masks.shape[1] // 8) * 8, LANES), F32),
        x_own=vmem((k, T, F), BF16),
        x_sib=vmem((k, T, F), BF16),
        j_own=vmem((k, T, W), F32),
        j_send=vmem((o, k, T, W), BF16),
        j_recv=vmem((o, k, T, W), BF16),
        st_own=vmem((k, 1, LANES), F32),
        st_recv=vmem((o, k, 1, LANES), F32),
        qkv=vmem((k, T, W), BF16),
        r_all=vmem((k, T, LANES), F32),
        probs=vmem((k, H // HEAD_DIM * T, T), F32),
        mixed=vmem((k, T, H), BF16),
        mixed_sib=vmem((k, T, H), BF16),
        y_own=vmem((k, T, F), F32),
        y_recv=vmem((o, k, T, F), BF16),
        y_send=vmem((o, k, T, F), BF16),
        z_send=vmem((k, T, F), BF16),
        u_all=vmem((n, k, T, F), BF16),
        g_all=vmem((n, k, T, W), BF16),
        gs_all=vmem((n, k, 1, LANES), F32),
        gm=vmem((k, T, H), BF16),
        gkv=vmem((k, T, W - H), BF16),
        normed=vmem((k, T, F), BF16),
        d_send=vmem((k, T, F), BF16),
        gain_acc=vmem((8, F), F32),
        gain_all=vmem((n, 1, F), F32),
        w_l=dma((2 * d.chips + 3,)),
        w_s=dma((2 * d.chips + 1,)),
        w_r=dma((2 * d.chips + 1,)),
        b_s=dma((n - 1,)),
        b_r=dma((n - 1,)),
        n_s=dma((n - 1,)),
        n_r=dma((n - 1,)),
        d_s=dma((d.mb, n - 1)),
        g_s=dma((d.mb, n - 1)),
        o_s=dma((5, k)),
    )
    for name in ("x_r", "u_r", "xs_s", "xs_r", "m_s", "m_r", "z_s", "dz_s"):
        scratch[name] = each
    for name in ("us_s", "us_r", "gs_s", "gs_r"):
        scratch[name] = each
    for name in ("j_s", "j_r", "st_s", "st_r", "y_s", "y_r", "ux_s", "ux_r", "ur_s", "ur_r", "gx_s", "gx_r", "gr_s", "gr_r"):
        scratch[name] = cross
    for name in ("hx_s", "hx_r"):
        scratch[name] = dma((n - 1, k))
    d.names = list(scratch)
    anywhere = pl.BlockSpec(memory_space=pl.ANY)
    inside = pl.BlockSpec(memory_space=pltpu.VMEM)
    rows = k * T
    kept = [(k, T, F), (k, T, H), (n, k, T, W), (k, T, W - H), (n, k, T, F)]
    *blocks, gain_all = pl.pallas_call(
        functools.partial(step_kernel, d),
        out_shape=[jax.ShapeDtypeStruct(shape, BF16) for shape in kept]
        + [jax.ShapeDtypeStruct((n, 1, F), F32)],
        in_specs=[anywhere, anywhere, pl.BlockSpec(memory_space=pltpu.SMEM), inside]
        + [anywhere] * 2,
        out_specs=[anywhere] * 5 + [inside],
        scratch_shapes=list(scratch.values()),
        compiler_params=pltpu.CompilerParams(
            collective_id=0, has_side_effects=True, vmem_limit_bytes=58 << 20
        ),
    )(stream, ograd, masks, gain, wj, wo)
    flat = [(rows, F), (rows, H), (n, rows, W), (rows, W - H), (n, rows, F)]
    return pl.pallas_call(
        functools.partial(weights_kernel, d),
        out_shape=[
            jax.ShapeDtypeStruct((F, J), F32),
            jax.ShapeDtypeStruct((H, d.D), F32),
            jax.ShapeDtypeStruct((1, n * F), F32),
        ],
        in_specs=[anywhere] * 5 + [inside],
        out_specs=[anywhere] * 2 + [inside],
        scratch_shapes=[vmem(shape, BF16) for shape in flat]
        + [vmem((F, J), F32), vmem((H, d.D), F32), dma((2 * n + 3,)), dma((2 * n + 1,))],
        compiler_params=pltpu.CompilerParams(vmem_limit_bytes=60 << 20),
    )(*[block.reshape(shape) for block, shape in zip(blocks, flat)], gain_all)


def body(stream_in, out_grad, mask_blocks, norm_gain, w_joined, w_out):
    n = lax.axis_size("dp")
    wj, wo = w_joined[0], w_out[0]
    mb = mask_blocks.shape[0]
    d = types.SimpleNamespace(
        n=n,
        S=lax.axis_size("section"),
        chips=n // CORES,
        mb=mb,
        k=mb * n,
        T=stream_in.shape[0] // mb,
        F=wj.shape[0],
        D=stream_in.shape[1],
    )
    real = wo.shape[0]
    d.H = -(-real // LANES) * LANES
    d.W = d.H + 2 * HEAD_DIM
    pad = d.H - real
    if pad:
        heads = wj[:, : n * real].reshape(d.F, n, real)
        heads = jnp.pad(heads, ((0, 0), (0, 0), (0, pad))).reshape(d.F, n * d.H)
        wj = jnp.concatenate([heads, wj[:, n * real :]], axis=1)
        wo = jnp.pad(wo, ((0, pad), (0, 0)))
    gj, go, gain = train_step(d, stream_in, out_grad, mask_blocks, norm_gain, wj, wo)
    if pad:
        heads = gj[:, : n * d.H].reshape(d.F, n, d.H)[:, :, :real].reshape(d.F, n * real)
        gj = jnp.concatenate([heads, gj[:, n * d.H :]], axis=1)
        go = go[:real]
    return gj[None], go[None], gain


def solution(mesh):
    return jax.shard_map(
        body,
        mesh=mesh,
        in_specs=(
            P(("groups", "dp"), None),
            P(("groups", "dp"), None),
            P(("groups", "dp"), None, None),
            P("section", None),
            P("section", "dp", None),
            P("section", "dp", None),
        ),
        out_specs=(
            P(("groups", "section"), "dp", None),
            P(("groups", "section"), "dp", None),
            P(("groups", "section"), None),
        ),
        check_vma=False,
    )
```

```python
import functools
import math
import types

import jax
import jax.numpy as jnp
from jax import lax
from jax.experimental import pallas as pl
from jax.experimental.pallas import tpu as pltpu
from jax.sharding import PartitionSpec as P

HEAD_DIM = 64
BLOCK_LEN = 16
LANES = 128
CORES = 2
EPSILON = 1e-05
F32 = jnp.float32
BF16 = jnp.bfloat16
NN = (((1,), (0,)), ((), ()))
NT = (((1,), (1,)), ((), ()))
TN = (((0,), (0,)), ((), ()))

LAG = dict(FA=0, F1=1, F2=3, F3=3, F4=5, BA=0, BR=1, BM=2, B1=2, GR=4, B3=5)
ORDER = ("B3", "F2", "GR", "BM", "BA", "F1", "B1", "F4", "BR", "FA", "F3")
FIRST_BACK = 1
STAGE_GAP = 13
VMEM = 60 << 20


def dot(left, right, dims=NN):
    return lax.dot_general(left, right, dims, preferred_element_type=F32)


def step_kernel(d, stream, ograd, masks, gain, wj, wo, *rest):
    outs, scratch = rest[:6], rest[6:]
    s = types.SimpleNamespace(**dict(zip(d.names, scratch)))
    s.normed, s.mixed, s.g_all, s.gkv, s.u_all, gain_out = outs
    n, k, T, F, H, W, chips = d.n, d.k, d.T, d.F, d.H, d.W, d.chips
    me = lax.axis_index("dp")
    sec = lax.axis_index("section")
    last = d.S - 1
    chip, core = me // CORES, lax.rem(me, CORES)
    sib = me + 1 - 2 * core
    others = range(1, chips)

    def ahead(kk):
        return lax.rem(chip + kk, chips) * CORES

    def behind(kk):
        return lax.rem(chip + chips - kk, chips) * CORES

    def push(src, dst, send, recv, device):
        pltpu.make_async_remote_copy(
            src_ref=src,
            dst_ref=dst,
            send_sem=send,
            recv_sem=recv,
            device_id=device,
            device_id_type=pl.DeviceIdType.MESH,
        ).start()

    def done(ref, sem):
        pltpu.make_async_copy(ref, ref, sem).wait()

    def cols(index, width):
        return pl.ds(pl.multiple_of(index * width, LANES), width)

    to_sib = {"dp": sib}

    def column(kk):
        return pl.ds(0, H) if kk == 0 else pl.ds(W + (kk - 1) * H, H)

    def pieces(which):
        out = []
        for kk in range(chips):
            e = ahead(kk) + which
            out.append((wj, cols(e, H), s.wjf, column(kk)))
        out.append((wj, pl.ds(n * H, W - H), s.wjf, pl.ds(H, W - H)))
        for kk in range(chips):
            e = ahead(kk) + which
            out.append((wo, cols(e, F), s.wof, pl.ds(kk * F, F)))
        return out

    loads = []
    for i, (src, there, dst, here) in enumerate(pieces(core)):
        rows = src.shape[0]
        loads.append(
            pltpu.make_async_copy(
                src.at[:, there], dst.at[pl.ds(0, rows), here], s.w_l.at[i]
            )
        )
    loads.append(pltpu.make_async_copy(wj, s.wj_own, s.w_l.at[2 * chips + 1]))
    loads.append(pltpu.make_async_copy(wo, s.wo_own, s.w_l.at[2 * chips + 2]))
    for copy in loads:
        copy.start()

    bias = s.bias_all.at[me]
    block_of = lax.broadcasted_iota(jnp.int32, (1, LANES), 1) // BLOCK_LEN
    for m in range(d.mb):
        for q in range(masks.shape[1]):
            hit = block_of == masks[m, q, 0]
            for j in range(1, masks.shape[2]):
                hit = jnp.logical_or(hit, block_of == masks[m, q, j])
            s.bias_all[me, m, q : q + 1, :] = jnp.where(hit, 0.0, -1e30)

    barrier = pltpu.get_barrier_semaphore()

    def greet(device):
        pl.semaphore_signal(
            barrier, inc=1, device_id=device, device_id_type=pl.DeviceIdType.MESH
        )

    for shift in range(1, n):
        greet({"dp": lax.rem(me + shift, n)})

    @pl.when(sec > 0)
    def _():
        greet({"section": sec - 1})

    @pl.when(sec < last)
    def _():
        greet({"section": sec + 1})

    ends = (sec > 0).astype(jnp.int32) + (sec < last).astype(jnp.int32)
    pl.semaphore_wait(barrier, n - 1 + ends)

    def local(src, dst, sem):
        pltpu.make_async_copy(src, dst, sem).start()

    @pl.when(sec == 0)
    def _():
        for i in range(d.mb):
            t = i * n + me
            rows = pl.ds(i * T, T)
            local(stream.at[rows, cols(me, F)], s.x_own.at[t], s.x_r.at[t])
            for shift in range(1, n):
                e = lax.rem(me + shift, n)
                push(
                    stream.at[rows, cols(e, F)],
                    s.x_own.at[t],
                    s.d_s.at[i, shift - 1],
                    s.x_r.at[t],
                    {"dp": e},
                )

    for i, (src, there, dst, here) in enumerate(pieces(1 - core)):
        rows = src.shape[0]
        push(
            src.at[:, there],
            dst.at[pl.ds(rows, rows), here],
            s.w_s.at[i],
            s.w_r.at[i],
            to_sib,
        )

    for shift in range(1, n):
        e = lax.rem(me + shift, n)
        push(bias, bias, s.b_s.at[shift - 1], s.b_r.at[shift - 1], {"dp": e})

    @pl.when(sec == last)
    def _():
        for i in range(d.mb):
            t = i * n + me
            rows = pl.ds(i * T, T)
            local(ograd.at[rows, cols(me, F)], s.u_all.at[me, t], s.u_r.at[t])
            for shift in range(1, n):
                e = lax.rem(me + shift, n)
                push(
                    ograd.at[rows, cols(e, F)],
                    s.u_all.at[e, t],
                    s.g_s.at[i, shift - 1],
                    s.u_r.at[t],
                    {"dp": e},
                )

    s.gain_acc[...] = jnp.zeros_like(s.gain_acc)
    for copy in loads:
        copy.wait()
    for i, (src, there, dst, here) in enumerate(pieces(core)):
        rows = src.shape[0]
        done(dst.at[pl.ds(rows, rows), here], s.w_r.at[i])
    for shift in range(1, n):
        done(s.bias_all.at[lax.rem(me + n - shift, n)], s.b_r.at[shift - 1])

    def eye():
        return lax.broadcasted_iota(jnp.int32, (T, LANES), 0) == lax.broadcasted_iota(
            jnp.int32, (T, LANES), 1
        )

    def to_row(column_values):
        return jnp.sum(jnp.where(eye(), column_values, 0.0), axis=0, keepdims=True)

    def to_column(row_values):
        return jnp.sum(
            jnp.where(eye(), jnp.broadcast_to(row_values, (T, LANES)), 0.0), axis=1, keepdims=True
        )

    def low_half(rows):
        return lax.broadcasted_iota(jnp.int32, (rows, LANES), 1) < HEAD_DIM

    def stack_heads(rows):
        low = low_half(T)
        out = []
        for pair in range(H // LANES):
            both = rows[:, pair * LANES : (pair + 1) * LANES]
            out += [jnp.where(low, both, 0.0), jnp.where(low, 0.0, both)]
        return jnp.concatenate(out, axis=0)

    def unstack_heads(rows):
        low = low_half(T)
        out = []
        for pair in range(H // LANES):
            first = rows[2 * pair * T : (2 * pair + 1) * T]
            second = rows[(2 * pair + 1) * T : (2 * pair + 2) * T]
            out.append(jnp.where(low, first, second))
        return jnp.concatenate(out, axis=1)

    def doubled(kv):
        low = low_half(T)
        turned = pltpu.roll(kv, HEAD_DIM, 1)
        return jnp.where(low, kv, turned).astype(BF16), jnp.where(low, turned, kv).astype(BF16)

    peers = [sib] + [ahead(kk) + c for kk in others for c in (core, 1 - core)]
    sources = [sib] + [behind(kk) + c for kk in others for c in (core, 1 - core)]
    g_own = gain[:, cols(me, F)]
    g_sib = gain[:, cols(sib, F)]

    def fa(t):
        done(s.x_own.at[t], s.x_r.at[t])
        push(s.x_own.at[t], s.x_sib.at[t], s.xs_s.at[t], s.xs_r.at[t], to_sib)

    def f1(t):
        own = s.x_own[t].astype(F32)
        done(s.x_sib.at[t], s.xs_r.at[t])
        beside = s.x_sib[t].astype(F32)
        squares = jnp.sum(own * own, axis=1, keepdims=True) + jnp.sum(
            beside * beside, axis=1, keepdims=True
        )
        part = dot((own * g_own).astype(BF16), s.wjf[:F]) + dot(
            (beside * g_sib).astype(BF16), s.wjf[F:]
        )
        s.j_own[t] = part[:, :W]
        s.st_own[t] = to_row(squares)
        for kk in others:
            s.j_send[kk - 1, t, :, :H] = part[:, W + (kk - 1) * H : W + kk * H].astype(BF16)
            s.j_send[kk - 1, t, :, H:] = part[:, H:W].astype(BF16)
        for kk in others:
            there = {"dp": ahead(kk) + core}
            at = (kk - 1, t)
            push(s.j_send.at[at], s.j_recv.at[at], s.j_s.at[at], s.j_r.at[at], there)
            push(s.st_own.at[t], s.st_recv.at[at], s.st_s.at[at], s.st_r.at[at], there)
        done(s.x_own.at[t], s.xs_s.at[t])

    def f2(t):
        total = s.j_own[t]
        squares = s.st_own[t]
        for kk in others:
            at = (kk - 1, t)
            done(s.j_recv.at[at], s.j_r.at[at])
            done(s.st_recv.at[at], s.st_r.at[at])
            total = total + s.j_recv[at].astype(F32)
            squares = squares + s.st_recv[at]
        inv_rms = lax.rsqrt(to_column(squares) / d.D + EPSILON)
        joined = (total * inv_rms).astype(BF16)
        s.qkv[t] = joined
        s.r_all[t] = jnp.broadcast_to(inv_rms, (T, LANES))
        wide = joined.astype(F32)
        queries = stack_heads(wide[:, :H]).astype(BF16)
        kk_rows, vv_rows = doubled(wide[:, H:])
        scores = dot(queries, kk_rows, NT) * HEAD_DIM ** (-0.5)
        blocks = s.bias_all[lax.rem(t, n), t // n]
        rows = [
            jnp.broadcast_to(blocks[b : b + 1, :T], (BLOCK_LEN, T)) for b in range(T // BLOCK_LEN)
        ]
        scores = scores + jnp.concatenate(rows * (H // HEAD_DIM), axis=0)
        exps = jnp.exp(scores - jnp.max(scores, axis=1, keepdims=True))
        probs = exps / jnp.sum(exps, axis=1, keepdims=True)
        s.probs[t] = probs
        s.mixed[t] = unstack_heads(dot(probs.astype(BF16), vv_rows)).astype(BF16)

        @pl.when(sec < last)
        def _():
            push(s.mixed.at[t], s.mixed_sib.at[t], s.m_s.at[t], s.m_r.at[t], to_sib)

        for kk in others:
            at = (kk - 1, t)
            done(s.j_send.at[at], s.j_s.at[at])
            done(s.st_own.at[t], s.st_s.at[at])

    def f3(t):
        @pl.when(sec < last)
        def _():
            done(s.mixed_sib.at[t], s.m_r.at[t])
            part = dot(s.mixed[t], s.wof[:H]) + dot(s.mixed_sib[t], s.wof[H:])
            for kk in others:
                at = (kk - 1, t)
                s.y_send[at] = part[:, kk * F : (kk + 1) * F].astype(BF16)
                push(
                    s.y_send.at[at],
                    s.y_recv.at[at],
                    s.y_s.at[at],
                    s.y_r.at[at],
                    {"dp": ahead(kk) + core},
                )
            s.y_own[t] = part[:, :F] + s.x_own[t].astype(F32)
            done(s.mixed.at[t], s.m_s.at[t])

    def f4(t):
        @pl.when(sec < last)
        def _():
            total = s.y_own[t]
            for kk in others:
                at = (kk - 1, t)
                done(s.y_recv.at[at], s.y_r.at[at])
                total = total + s.y_recv[at].astype(F32)
            s.z_send[t] = total.astype(BF16)
            push(s.z_send.at[t], s.x_own.at[t], s.z_s.at[t], s.x_r.at[t], {"section": sec + 1})
            for kk in others:
                done(s.y_send.at[kk - 1, t], s.y_s.at[kk - 1, t])

    def ba(t):
        mine = s.u_all.at[me, t]
        done(mine, s.u_r.at[t])
        for kk in others:
            at = (kk - 1, t)
            push(mine, mine, s.ux_s.at[at], s.ux_r.at[at], {"dp": ahead(kk) + core})
        push(mine, mine, s.us_s.at[t], s.us_r.at[t], to_sib)

    def br(t):
        for kk in others:
            at = (kk - 1, t)
            block = s.u_all.at[behind(kk) + core, t]
            done(block, s.ux_r.at[at])
            push(block, block, s.ur_s.at[at], s.ur_r.at[at], to_sib)

    def bm(t):
        done(s.u_all.at[sib, t], s.us_r.at[t])
        for kk in others:
            done(s.u_all.at[behind(kk) + 1 - core, t], s.ur_r.at[kk - 1, t])
        upstream = jnp.concatenate([s.u_all[e, t] for e in range(n)], axis=1)
        s.gm[t] = dot(upstream, s.wo_own[...], NT).astype(BF16)
        done(s.u_all.at[me, t], s.us_s.at[t])
        for kk in others:
            done(s.u_all.at[me, t], s.ux_s.at[kk - 1, t])
            done(s.u_all.at[behind(kk) + core, t], s.ur_s.at[kk - 1, t])

    def b1(t):
        grads = stack_heads(s.gm[t].astype(F32)).astype(BF16)
        joined = s.qkv[t].astype(F32)
        queries = stack_heads(joined[:, :H]).astype(BF16)
        kk_rows, vv_rows = doubled(joined[:, H:])
        probs = s.probs[t]
        grad_probs = dot(grads, vv_rows, NT)
        inner = jnp.sum(probs * grad_probs, axis=1, keepdims=True)
        grad_scores = (probs * (grad_probs - inner) * HEAD_DIM ** (-0.5)).astype(BF16)
        grad_values = dot(probs.astype(BF16), grads, TN)
        grad_keys = dot(grad_scores, queries, TN)
        grad_queries = unstack_heads(dot(grad_scores, kk_rows))
        grad_kv = jnp.where(
            low_half(T),
            grad_keys + pltpu.roll(grad_keys, HEAD_DIM, 1),
            grad_values + pltpu.roll(grad_values, HEAD_DIM, 1),
        )
        message = jnp.concatenate([grad_queries, grad_kv], axis=1)
        s.g_all[me, t] = message.astype(BF16)
        s.gs_all[me, t] = to_row(jnp.sum(message * joined, axis=1, keepdims=True))
        mine, stat = s.g_all.at[me, t], s.gs_all.at[me, t]
        for kk in others:
            at = (kk - 1, t)
            push(mine, mine, s.gx_s.at[at], s.gx_r.at[at], {"dp": ahead(kk) + core})
        push(mine, mine, s.gs_s.at[t], s.gs_r.at[t], to_sib)
        for shift, e in enumerate(peers):
            at = (shift, t)
            push(stat, stat, s.hx_s.at[at], s.hx_r.at[at], {"dp": e})

    def gr(t):
        for kk in others:
            at = (kk - 1, t)
            block = s.g_all.at[behind(kk) + core, t]
            done(block, s.gx_r.at[at])
            push(block, block, s.gr_s.at[at], s.gr_r.at[at], to_sib)

    def b3(t):
        done(s.g_all.at[sib, t], s.gs_r.at[t])
        for kk in others:
            done(s.g_all.at[behind(kk) + 1 - core, t], s.gr_r.at[kk - 1, t])
        for shift, e in enumerate(sources):
            done(s.gs_all.at[e, t], s.hx_r.at[shift, t])
        blocks = [s.g_all[e, t] for e in range(n)]
        grad_kv = functools.reduce(lambda a, b: a + b, [b[:, H:].astype(F32) for b in blocks])
        grad_kv = grad_kv.astype(BF16)
        s.gkv[t] = grad_kv
        rows = jnp.concatenate([b[:, :H] for b in blocks] + [grad_kv], axis=1)
        grad_normed = dot(rows, s.wj_own[...], NT)
        stat = functools.reduce(lambda a, b: a + b, [s.gs_all[e, t] for e in range(n)])
        inv_rms = s.r_all[t][:, :1]
        wide = s.x_own[t].astype(F32)
        scaled = wide * inv_rms
        s.normed[t] = (scaled * g_own).astype(BF16)
        s.gain_acc[...] += jnp.sum((grad_normed * scaled).reshape(T // 8, 8, F), axis=0)

        @pl.when(sec > 0)
        def _():
            mean = to_column(stat) / d.D
            down = s.u_all[me, t].astype(F32) + inv_rms * (g_own * grad_normed - scaled * mean)
            s.d_send[t] = down.astype(BF16)
            push(
                s.d_send.at[t], s.u_all.at[me, t], s.dz_s.at[t], s.u_r.at[t], {"section": sec - 1}
            )

        done(s.g_all.at[me, t], s.gs_s.at[t])
        for kk in others:
            done(s.g_all.at[me, t], s.gx_s.at[kk - 1, t])
            done(s.g_all.at[behind(kk) + core, t], s.gr_s.at[kk - 1, t])
        for shift in range(n - 1):
            done(s.gs_all.at[me, t], s.hx_s.at[shift, t])

    @pl.when(sec == last)
    def _():
        for phase in (ba, br, bm):
            lax.fori_loop(0, k, lambda t, c, phase=phase: (phase(t), c)[1], 0)

    phases = dict(FA=fa, F1=f1, F2=f2, F3=f3, F4=f4, BA=ba, BR=br, BM=bm, B1=b1, GR=gr, B3=b3)
    gap = jnp.minimum(FIRST_BACK + STAGE_GAP * (last - sec), k + LAG["F4"])

    def step(now, carry):
        for name in ORDER:
            t = now - LAG[name] - (gap if name[0] != "F" else 0)
            run = jnp.logical_and(t >= 0, t < k)
            if name in ("BA", "BR", "BM"):
                run = jnp.logical_and(run, sec < last)

            @pl.when(run)
            def _(name=name, t=t):
                phases[name](t)

        return carry

    lax.fori_loop(0, k + jnp.maximum(gap + LAG["B3"], LAG["F4"]), step, 0)

    s.gain_all[me] = jnp.sum(s.gain_acc[...], axis=0, keepdims=True)
    for shift in range(1, n):
        push(
            s.gain_all.at[me],
            s.gain_all.at[me],
            s.n_s.at[shift - 1],
            s.n_r.at[shift - 1],
            {"dp": lax.rem(me + shift, n)},
        )
    for shift in range(1, n):
        done(s.gain_all.at[lax.rem(me + n - shift, n)], s.n_r.at[shift - 1])
        done(s.gain_all.at[me], s.n_s.at[shift - 1])
    gain_out[...] = s.gain_all[...]

    @pl.when(sec == 0)
    def _():
        for i in range(d.mb):
            for shift in range(n - 1):
                done(stream.at[pl.ds(i * T, T), pl.ds(0, F)], s.d_s.at[i, shift])

    @pl.when(sec == last)
    def _():
        for i in range(d.mb):
            for shift in range(n - 1):
                done(ograd.at[pl.ds(i * T, T), pl.ds(0, F)], s.g_s.at[i, shift])

    for i, (src, there, dst, here) in enumerate(pieces(1 - core)):
        done(src.at[:, there], s.w_s.at[i])
    for shift in range(1, n):
        done(bias, s.b_s.at[shift - 1])

    def settle(t, carry):
        @pl.when(sec < last)
        def _():
            done(s.z_send.at[t], s.z_s.at[t])

        @pl.when(sec > 0)
        def _():
            done(s.d_send.at[t], s.dz_s.at[t])

        return carry

    lax.fori_loop(0, k, settle, 0)


def weights_kernel(d, normed_in, mixed_in, g_in, gkv_in, u_in, gain_in, *rest):
    gj_out, go_out, gain_out, gj, go, out_sems = rest
    n, F, H = d.n, d.F, d.H
    stores = []

    def store(block, out, start, width):
        here = (slice(None), pl.ds(start, width))
        copy = pltpu.make_async_copy(block.at[here], out.at[here], out_sems.at[len(stores)])
        copy.start()
        stores.append(copy)

    gain_out[...] = jnp.concatenate([gain_in[e] for e in range(n)], axis=1)
    for e in range(n):
        gj[:, e * H : (e + 1) * H] = dot(normed_in[...], g_in[e, :, :H], TN)
        store(gj, gj_out, e * H, H)
        go[:, e * F : (e + 1) * F] = dot(mixed_in[...], u_in[e], TN)
        store(go, go_out, e * F, F)
    gj[:, n * H :] = dot(normed_in[...], gkv_in[...], TN)
    store(gj, gj_out, n * H, d.W - H)
    for copy in stores:
        copy.wait()


def train_step(d, stream, ograd, masks, gain, wj, wo):
    n, k, T, F, H, W = d.n, d.k, d.T, d.F, d.H, d.W
    o = d.chips - 1
    J = n * H + W - H
    vmem, dma = pltpu.VMEM, pltpu.SemaphoreType.DMA
    each, cross = dma((k,)), dma((o, k))
    scratch = dict(
        wjf=vmem((2 * F, W + o * H), BF16),
        wof=vmem((2 * H, d.chips * F), BF16),
        wj_own=vmem((F, J), BF16),
        wo_own=vmem((H, d.D), BF16),
        bias_all=vmem((n, d.mb, -(-masks.shape[1] // 8) * 8, LANES), F32),
        x_own=vmem((k, T, F), BF16),
        x_sib=vmem((k, T, F), BF16),
        j_own=vmem((k, T, W), F32),
        j_send=vmem((o, k, T, W), BF16),
        j_recv=vmem((o, k, T, W), BF16),
        st_own=vmem((k, 1, LANES), F32),
        st_recv=vmem((o, k, 1, LANES), F32),
        qkv=vmem((k, T, W), BF16),
        r_all=vmem((k, T, LANES), F32),
        probs=vmem((k, H // HEAD_DIM * T, T), F32),
        mixed_sib=vmem((k, T, H), BF16),
        y_own=vmem((k, T, F), F32),
        y_recv=vmem((o, k, T, F), BF16),
        y_send=vmem((o, k, T, F), BF16),
        z_send=vmem((k, T, F), BF16),
        gs_all=vmem((n, k, 1, LANES), F32),
        gm=vmem((k, T, H), BF16),
        d_send=vmem((k, T, F), BF16),
        gain_acc=vmem((8, F), F32),
        gain_all=vmem((n, 1, F), F32),
        w_l=dma((2 * d.chips + 3,)),
        w_s=dma((2 * d.chips + 1,)),
        w_r=dma((2 * d.chips + 1,)),
        b_s=dma((n - 1,)),
        b_r=dma((n - 1,)),
        n_s=dma((n - 1,)),
        n_r=dma((n - 1,)),
        d_s=dma((d.mb, n - 1)),
        g_s=dma((d.mb, n - 1)),
    )
    for name in ("x_r", "u_r", "xs_s", "xs_r", "m_s", "m_r", "z_s", "dz_s"):
        scratch[name] = each
    for name in ("us_s", "us_r", "gs_s", "gs_r"):
        scratch[name] = each
    for name in ("j_s", "j_r", "st_s", "st_r", "y_s", "y_r", "ux_s", "ux_r", "ur_s", "ur_r", "gx_s", "gx_r", "gr_s", "gr_r"):
        scratch[name] = cross
    for name in ("hx_s", "hx_r"):
        scratch[name] = dma((n - 1, k))
    d.names = list(scratch)
    anywhere = pl.BlockSpec(memory_space=pl.ANY)
    inside = pl.BlockSpec(memory_space=pltpu.VMEM)
    rows = k * T
    kept = [(k, T, F), (k, T, H), (n, k, T, W), (k, T, W - H), (n, k, T, F)]
    kept_bytes = 2 * sum(math.prod(shape) for shape in kept)
    *blocks, gain_all = pl.pallas_call(
        functools.partial(step_kernel, d),
        out_shape=[pltpu.VMEM(shape, BF16) for shape in kept]
        + [jax.ShapeDtypeStruct((n, 1, F), F32)],
        in_specs=[anywhere, anywhere, pl.BlockSpec(memory_space=pltpu.SMEM), inside]
        + [anywhere] * 2,
        out_specs=[inside] * 6,
        scratch_shapes=list(scratch.values()),
        compiler_params=pltpu.CompilerParams(
            collective_id=0, has_side_effects=True, vmem_limit_bytes=VMEM - kept_bytes
        ),
    )(stream, ograd, masks, gain, wj, wo)
    flat = [(rows, F), (rows, H), (n, rows, W), (rows, W - H), (n, rows, F)]
    return pl.pallas_call(
        functools.partial(weights_kernel, d),
        out_shape=[
            jax.ShapeDtypeStruct((F, J), F32),
            jax.ShapeDtypeStruct((H, d.D), F32),
            jax.ShapeDtypeStruct((1, n * F), F32),
        ],
        in_specs=[inside] * 6,
        out_specs=[anywhere] * 2 + [inside],
        scratch_shapes=[vmem((F, J), F32), vmem((H, d.D), F32), dma((2 * n + 1,))],
        compiler_params=pltpu.CompilerParams(vmem_limit_bytes=VMEM // 2),
    )(*[block.reshape(shape) for block, shape in zip(blocks, flat)], gain_all)


def body(stream_in, out_grad, mask_blocks, norm_gain, w_joined, w_out):
    n = lax.axis_size("dp")
    wj, wo = w_joined[0], w_out[0]
    mb = mask_blocks.shape[0]
    d = types.SimpleNamespace(
        n=n,
        S=lax.axis_size("section"),
        chips=n // CORES,
        mb=mb,
        k=mb * n,
        T=stream_in.shape[0] // mb,
        F=wj.shape[0],
        D=stream_in.shape[1],
    )
    real = wo.shape[0]
    d.H = -(-real // LANES) * LANES
    d.W = d.H + 2 * HEAD_DIM
    pad = d.H - real
    if pad:
        heads = wj[:, : n * real].reshape(d.F, n, real)
        heads = jnp.pad(heads, ((0, 0), (0, 0), (0, pad))).reshape(d.F, n * d.H)
        wj = jnp.concatenate([heads, wj[:, n * real :]], axis=1)
        wo = jnp.pad(wo, ((0, pad), (0, 0)))
    gj, go, gain = train_step(d, stream_in, out_grad, mask_blocks, norm_gain, wj, wo)
    if pad:
        heads = gj[:, : n * d.H].reshape(d.F, n, d.H)[:, :, :real].reshape(d.F, n * real)
        gj = jnp.concatenate([heads, gj[:, n * d.H :]], axis=1)
        go = go[:real]
    return gj[None], go[None], gain


def solution(mesh):
    return jax.shard_map(
        body,
        mesh=mesh,
        in_specs=(
            P(("groups", "dp"), None),
            P(("groups", "dp"), None),
            P(("groups", "dp"), None, None),
            P("section", None),
            P("section", "dp", None),
            P("section", "dp", None),
        ),
        out_specs=(
            P(("groups", "section"), "dp", None),
            P(("groups", "section"), "dp", None),
            P(("groups", "section"), None),
        ),
        check_vma=False,
    )
```

```python
import functools
import math
import types

import jax
import jax.numpy as jnp
from jax import lax
from jax.experimental import pallas as pl
from jax.experimental.pallas import tpu as pltpu
from jax.sharding import PartitionSpec as P

HEAD_DIM = 64
BLOCK_LEN = 16
LANES = 128
CORES = 2
EPSILON = 1e-05
F32 = jnp.float32
BF16 = jnp.bfloat16
NN = (((1,), (0,)), ((), ()))
NT = (((1,), (1,)), ((), ()))
TN = (((0,), (0,)), ((), ()))

LAG = dict(FA=0, F1=1, F2=3, F3=3, F4=5, BA=0, BR=1, BM=2, B1=2, GR=4, B3=5)
ORDER = ("B3", "F2", "GR", "BA", "F1", "BM", "B1", "F4", "F3", "FA", "BR")
FIRST_BACK = 1
STAGE_GAP = 13
VMEM = 60 << 20


def dot(left, right, dims=NN):
    return lax.dot_general(left, right, dims, preferred_element_type=F32)


def step_kernel(d, stream, ograd, masks, gain, wj, wo, *rest):
    outs, scratch = rest[:7], rest[7:]
    s = types.SimpleNamespace(**dict(zip(d.names, scratch)))
    s.normed, s.mixed, s.g_all, s.gkv, s.u_all, go_out, gain_out = outs
    n, k, T, F, H, W, chips = d.n, d.k, d.T, d.F, d.H, d.W, d.chips
    me = lax.axis_index("dp")
    sec = lax.axis_index("section")
    last = d.S - 1
    chip, core = me // CORES, lax.rem(me, CORES)
    sib = me + 1 - 2 * core
    others = range(1, chips)

    def ahead(kk):
        return lax.rem(chip + kk, chips) * CORES

    def behind(kk):
        return lax.rem(chip + chips - kk, chips) * CORES

    def push(src, dst, send, recv, device):
        pltpu.make_async_remote_copy(
            src_ref=src,
            dst_ref=dst,
            send_sem=send,
            recv_sem=recv,
            device_id=device,
            device_id_type=pl.DeviceIdType.MESH,
        ).start()

    def done(ref, sem):
        pltpu.make_async_copy(ref, ref, sem).wait()

    def cols(index, width):
        return pl.ds(pl.multiple_of(index * width, LANES), width)

    to_sib = {"dp": sib}

    def column(kk):
        return pl.ds(0, H) if kk == 0 else pl.ds(W + (kk - 1) * H, H)

    def pieces(which):
        out = []
        for kk in range(chips):
            e = ahead(kk) + which
            out.append((wj, cols(e, H), s.wjf, column(kk)))
        out.append((wj, pl.ds(n * H, W - H), s.wjf, pl.ds(H, W - H)))
        for kk in range(chips):
            e = ahead(kk) + which
            out.append((wo, cols(e, F), s.wof, pl.ds(kk * F, F)))
        return out

    loads = []
    for i, (src, there, dst, here) in enumerate(pieces(core)):
        rows = src.shape[0]
        loads.append(
            pltpu.make_async_copy(
                src.at[:, there], dst.at[pl.ds(0, rows), here], s.w_l.at[i]
            )
        )
    loads.append(pltpu.make_async_copy(wj, s.wj_own, s.w_l.at[2 * chips + 1]))
    loads.append(pltpu.make_async_copy(wo, s.wo_own, s.w_l.at[2 * chips + 2]))
    urgent = chips + 1
    for copy in loads[:urgent]:
        copy.start()

    bias = s.bias_all.at[me]
    block_of = lax.broadcasted_iota(jnp.int32, (1, LANES), 1) // BLOCK_LEN
    for m in range(d.mb):
        for q in range(masks.shape[1]):
            hit = block_of == masks[m, q, 0]
            for j in range(1, masks.shape[2]):
                hit = jnp.logical_or(hit, block_of == masks[m, q, j])
            s.bias_all[me, m, q : q + 1, :] = jnp.where(hit, 0.0, -1e30)

    barrier = pltpu.get_barrier_semaphore()

    def greet(device):
        pl.semaphore_signal(
            barrier, inc=1, device_id=device, device_id_type=pl.DeviceIdType.MESH
        )

    for shift in range(1, n):
        greet({"dp": lax.rem(me + shift, n)})

    @pl.when(sec > 0)
    def _():
        greet({"section": sec - 1})

    @pl.when(sec < last)
    def _():
        greet({"section": sec + 1})

    ends = (sec > 0).astype(jnp.int32) + (sec < last).astype(jnp.int32)
    pl.semaphore_wait(barrier, n - 1 + ends)

    def local(src, dst, sem):
        pltpu.make_async_copy(src, dst, sem).start()

    @pl.when(sec == 0)
    def _():
        for i in range(d.mb):
            t = i * n + me
            rows = pl.ds(i * T, T)
            local(stream.at[rows, cols(me, F)], s.x_own.at[t], s.x_r.at[t])
            for shift in range(1, n):
                e = lax.rem(me + shift, n)
                push(
                    stream.at[rows, cols(e, F)],
                    s.x_own.at[t],
                    s.d_s.at[i, shift - 1],
                    s.x_r.at[t],
                    {"dp": e},
                )

    for i, (src, there, dst, here) in enumerate(pieces(1 - core)):
        rows = src.shape[0]
        push(
            src.at[:, there],
            dst.at[pl.ds(rows, rows), here],
            s.w_s.at[i],
            s.w_r.at[i],
            to_sib,
        )
    for copy in loads[urgent:]:
        copy.start()

    for shift in range(1, n):
        e = lax.rem(me + shift, n)
        push(bias, bias, s.b_s.at[shift - 1], s.b_r.at[shift - 1], {"dp": e})

    @pl.when(sec == last)
    def _():
        for i in range(d.mb):
            t = i * n + me
            rows = pl.ds(i * T, T)
            local(ograd.at[rows, cols(me, F)], s.u_all.at[me, t], s.u_r.at[t])
            for shift in range(1, n):
                e = lax.rem(me + shift, n)
                push(
                    ograd.at[rows, cols(e, F)],
                    s.u_all.at[e, t],
                    s.g_s.at[i, shift - 1],
                    s.u_r.at[t],
                    {"dp": e},
                )

    s.gain_acc[...] = jnp.zeros_like(s.gain_acc)
    def pieces_here(begin, end):
        for i, (src, there, dst, here) in list(enumerate(pieces(core)))[begin:end]:
            rows = src.shape[0]
            loads[i].wait()
            done(dst.at[pl.ds(rows, rows), here], s.w_r.at[i])

    def masks_here():
        for shift in range(1, n):
            done(s.bias_all.at[lax.rem(me + n - shift, n)], s.b_r.at[shift - 1])

    def turn_weights():
        for copy in loads[2 * chips + 1 :]:
            copy.wait()
        s.wo_turned[...] = s.wo_own[...].T
        s.wj_turned[...] = s.wj_own[...].T

    @pl.when(sec > 0)
    def _():
        turn_weights()

    @pl.when(sec == last)
    def _():
        pieces_here(urgent, 2 * chips + 1)

    pieces_here(0, urgent)

    def eye():
        return lax.broadcasted_iota(jnp.int32, (T, LANES), 0) == lax.broadcasted_iota(
            jnp.int32, (T, LANES), 1
        )

    def to_row(column_values):
        return jnp.sum(jnp.where(eye(), column_values, 0.0), axis=0, keepdims=True)

    def to_column(row_values):
        return jnp.sum(
            jnp.where(eye(), jnp.broadcast_to(row_values, (T, LANES)), 0.0), axis=1, keepdims=True
        )

    def low_half(rows):
        return lax.broadcasted_iota(jnp.int32, (rows, LANES), 1) < HEAD_DIM

    def stack_heads(rows):
        low = low_half(T)
        out = []
        for pair in range(H // LANES):
            both = rows[:, pair * LANES : (pair + 1) * LANES]
            out += [jnp.where(low, both, 0.0), jnp.where(low, 0.0, both)]
        return jnp.concatenate(out, axis=0)

    def unstack_heads(rows):
        low = low_half(T)
        out = []
        for pair in range(H // LANES):
            first = rows[2 * pair * T : (2 * pair + 1) * T]
            second = rows[(2 * pair + 1) * T : (2 * pair + 2) * T]
            out.append(jnp.where(low, first, second))
        return jnp.concatenate(out, axis=1)

    def doubled(kv):
        low = low_half(T)
        turned = pltpu.roll(kv, HEAD_DIM, 1)
        return jnp.where(low, kv, turned).astype(BF16), jnp.where(low, turned, kv).astype(BF16)

    peers = [sib] + [ahead(kk) + c for kk in others for c in (core, 1 - core)]
    sources = [sib] + [behind(kk) + c for kk in others for c in (core, 1 - core)]
    g_own = gain[:, cols(me, F)]
    g_sib = gain[:, cols(sib, F)]

    def fa(t):
        done(s.x_own.at[t], s.x_r.at[t])
        push(s.x_own.at[t], s.x_sib.at[t], s.xs_s.at[t], s.xs_r.at[t], to_sib)

    def f1(t):
        own = s.x_own[t].astype(F32)
        done(s.x_sib.at[t], s.xs_r.at[t])
        beside = s.x_sib[t].astype(F32)
        squares = jnp.sum(own * own, axis=1, keepdims=True) + jnp.sum(
            beside * beside, axis=1, keepdims=True
        )
        part = dot((own * g_own).astype(BF16), s.wjf[:F]) + dot(
            (beside * g_sib).astype(BF16), s.wjf[F:]
        )
        s.j_own[t] = part[:, :W]
        s.st_own[t] = to_row(squares)
        for kk in others:
            s.j_send[kk - 1, t, :, :H] = part[:, W + (kk - 1) * H : W + kk * H].astype(BF16)
            s.j_send[kk - 1, t, :, H:] = part[:, H:W].astype(BF16)
        for kk in others:
            there = {"dp": ahead(kk) + core}
            at = (kk - 1, t)
            push(s.j_send.at[at], s.j_recv.at[at], s.j_s.at[at], s.j_r.at[at], there)
            push(s.st_own.at[t], s.st_recv.at[at], s.st_s.at[at], s.st_r.at[at], there)
        done(s.x_own.at[t], s.xs_s.at[t])

    def f2(t):
        total = s.j_own[t]
        squares = s.st_own[t]
        for kk in others:
            at = (kk - 1, t)
            done(s.j_recv.at[at], s.j_r.at[at])
            done(s.st_recv.at[at], s.st_r.at[at])
            total = total + s.j_recv[at].astype(F32)
            squares = squares + s.st_recv[at]
        pl.when(t == 0)(masks_here)
        inv_rms = lax.rsqrt(to_column(squares) / d.D + EPSILON)
        joined = (total * inv_rms).astype(BF16)
        s.qkv[t] = joined
        s.r_all[t] = jnp.broadcast_to(inv_rms, (T, LANES))
        wide = joined.astype(F32)
        queries = stack_heads(wide[:, :H]).astype(BF16)
        kk_rows, vv_rows = doubled(wide[:, H:])
        scores = dot(queries, kk_rows, NT) * HEAD_DIM ** (-0.5)
        blocks = s.bias_all[lax.rem(t, n), t // n]
        rows = [
            jnp.broadcast_to(blocks[b : b + 1, :T], (BLOCK_LEN, T)) for b in range(T // BLOCK_LEN)
        ]
        scores = scores + jnp.concatenate(rows * (H // HEAD_DIM), axis=0)
        exps = jnp.exp(scores - jnp.max(scores, axis=1, keepdims=True))
        probs = exps / jnp.sum(exps, axis=1, keepdims=True)
        s.probs[t] = probs
        s.mixed[t] = unstack_heads(dot(probs.astype(BF16), vv_rows)).astype(BF16)

        @pl.when(sec < last)
        def _():
            push(s.mixed.at[t], s.mixed_sib.at[t], s.m_s.at[t], s.m_r.at[t], to_sib)

        for kk in others:
            at = (kk - 1, t)
            done(s.j_send.at[at], s.j_s.at[at])
            done(s.st_own.at[t], s.st_s.at[at])

    def f3(t):
        @pl.when(sec < last)
        def _():
            done(s.mixed_sib.at[t], s.m_r.at[t])
            pl.when(t == 0)(lambda: pieces_here(urgent, 2 * chips + 1))
            part = dot(s.mixed[t], s.wof[:H]) + dot(s.mixed_sib[t], s.wof[H:])
            for kk in others:
                at = (kk - 1, t)
                s.y_send[at] = part[:, kk * F : (kk + 1) * F].astype(BF16)
                push(
                    s.y_send.at[at],
                    s.y_recv.at[at],
                    s.y_s.at[at],
                    s.y_r.at[at],
                    {"dp": ahead(kk) + core},
                )
            s.y_own[t] = part[:, :F] + s.x_own[t].astype(F32)
            done(s.mixed.at[t], s.m_s.at[t])

    def f4(t):
        @pl.when(sec < last)
        def _():
            total = s.y_own[t]
            for kk in others:
                at = (kk - 1, t)
                done(s.y_recv.at[at], s.y_r.at[at])
                total = total + s.y_recv[at].astype(F32)
            s.z_send[t] = total.astype(BF16)
            push(s.z_send.at[t], s.x_own.at[t], s.z_s.at[t], s.x_r.at[t], {"section": sec + 1})
            for kk in others:
                done(s.y_send.at[kk - 1, t], s.y_s.at[kk - 1, t])

    def ba(t):
        mine = s.u_all.at[me, t]
        done(mine, s.u_r.at[t])
        for kk in others:
            at = (kk - 1, t)
            push(mine, mine, s.ux_s.at[at], s.ux_r.at[at], {"dp": ahead(kk) + core})
        push(mine, mine, s.us_s.at[t], s.us_r.at[t], to_sib)

    def br(t):
        for kk in others:
            at = (kk - 1, t)
            block = s.u_all.at[behind(kk) + core, t]
            done(block, s.ux_r.at[at])
            push(block, block, s.ur_s.at[at], s.ur_r.at[at], to_sib)

    def bm(t):
        done(s.u_all.at[sib, t], s.us_r.at[t])
        for kk in others:
            done(s.u_all.at[behind(kk) + 1 - core, t], s.ur_r.at[kk - 1, t])
        upstream = jnp.concatenate([s.u_all[e, t] for e in range(n)], axis=1)
        s.gm[t] = dot(upstream, s.wo_turned[...]).astype(BF16)
        done(s.u_all.at[me, t], s.us_s.at[t])
        for kk in others:
            done(s.u_all.at[me, t], s.ux_s.at[kk - 1, t])
            done(s.u_all.at[behind(kk) + core, t], s.ur_s.at[kk - 1, t])

    def b1(t):
        grads = stack_heads(s.gm[t].astype(F32)).astype(BF16)
        joined = s.qkv[t].astype(F32)
        queries = stack_heads(joined[:, :H]).astype(BF16)
        kk_rows, vv_rows = doubled(joined[:, H:])
        probs = s.probs[t]
        grad_probs = dot(grads, vv_rows, NT)
        inner = jnp.sum(probs * grad_probs, axis=1, keepdims=True)
        grad_scores = (probs * (grad_probs - inner) * HEAD_DIM ** (-0.5)).astype(BF16)
        grad_values = dot(probs.astype(BF16), grads, TN)
        grad_keys = dot(grad_scores, queries, TN)
        grad_queries = unstack_heads(dot(grad_scores, kk_rows))
        grad_kv = jnp.where(
            low_half(T),
            grad_keys + pltpu.roll(grad_keys, HEAD_DIM, 1),
            grad_values + pltpu.roll(grad_values, HEAD_DIM, 1),
        )
        message = jnp.concatenate([grad_queries, grad_kv], axis=1)
        s.g_all[me, t] = message.astype(BF16)
        s.gs_all[me, t] = to_row(jnp.sum(message * joined, axis=1, keepdims=True))
        mine, stat = s.g_all.at[me, t], s.gs_all.at[me, t]
        for kk in others:
            at = (kk - 1, t)
            push(mine, mine, s.gx_s.at[at], s.gx_r.at[at], {"dp": ahead(kk) + core})
        push(mine, mine, s.gs_s.at[t], s.gs_r.at[t], to_sib)
        for shift, e in enumerate(peers):
            at = (shift, t)
            push(stat, stat, s.hx_s.at[at], s.hx_r.at[at], {"dp": e})

    def gr(t):
        for kk in others:
            at = (kk - 1, t)
            block = s.g_all.at[behind(kk) + core, t]
            done(block, s.gx_r.at[at])
            push(block, block, s.gr_s.at[at], s.gr_r.at[at], to_sib)

    def b3(t):
        done(s.g_all.at[sib, t], s.gs_r.at[t])
        for kk in others:
            done(s.g_all.at[behind(kk) + 1 - core, t], s.gr_r.at[kk - 1, t])
        for shift, e in enumerate(sources):
            done(s.gs_all.at[e, t], s.hx_r.at[shift, t])
        blocks = [s.g_all[e, t] for e in range(n)]
        grad_kv = functools.reduce(lambda a, b: a + b, [b[:, H:].astype(F32) for b in blocks])
        grad_kv = grad_kv.astype(BF16)
        s.gkv[t] = grad_kv
        rows = jnp.concatenate([b[:, :H] for b in blocks] + [grad_kv], axis=1)
        grad_normed = dot(rows, s.wj_turned[...])
        stat = functools.reduce(lambda a, b: a + b, [s.gs_all[e, t] for e in range(n)])
        inv_rms = s.r_all[t][:, :1]
        wide = s.x_own[t].astype(F32)
        scaled = wide * inv_rms
        s.normed[t] = (scaled * g_own).astype(BF16)
        s.gain_acc[...] += jnp.sum((grad_normed * scaled).reshape(T // 8, 8, F), axis=0)

        @pl.when(sec > 0)
        def _():
            mean = to_column(stat) / d.D
            down = s.u_all[me, t].astype(F32) + inv_rms * (g_own * grad_normed - scaled * mean)
            s.d_send[t] = down.astype(BF16)
            push(
                s.d_send.at[t], s.u_all.at[me, t], s.dz_s.at[t], s.u_r.at[t], {"section": sec - 1}
            )

        done(s.g_all.at[me, t], s.gs_s.at[t])
        for kk in others:
            done(s.g_all.at[me, t], s.gx_s.at[kk - 1, t])
            done(s.g_all.at[behind(kk) + core, t], s.gr_s.at[kk - 1, t])
        for shift in range(n - 1):
            done(s.gs_all.at[me, t], s.hx_s.at[shift, t])

    @pl.when(sec == last)
    def _():
        for phase in (ba, br, bm):
            lax.fori_loop(0, k, lambda t, c, phase=phase: (phase(t), c)[1], 0)

    phases = dict(FA=fa, F1=f1, F2=f2, F3=f3, F4=f4, BA=ba, BR=br, BM=bm, B1=b1, GR=gr, B3=b3)
    gap = jnp.minimum(FIRST_BACK + STAGE_GAP * (last - sec), k + LAG["F4"])

    def step(now, carry):
        pl.when(jnp.logical_and(sec == 0, now == k))(turn_weights)
        for name in ORDER:
            t = now - LAG[name] - (gap if name[0] != "F" else 0)
            run = jnp.logical_and(t >= 0, t < k)
            if name in ("BA", "BR", "BM"):
                run = jnp.logical_and(run, sec < last)

            @pl.when(run)
            def _(name=name, t=t):
                phases[name](t)

        return carry

    lax.fori_loop(0, k + jnp.maximum(gap + LAG["B3"], LAG["F4"]), step, 0)

    s.gain_all[me] = jnp.sum(s.gain_acc[...], axis=0, keepdims=True)
    for shift in range(1, n):
        push(
            s.gain_all.at[me],
            s.gain_all.at[me],
            s.n_s.at[shift - 1],
            s.n_r.at[shift - 1],
            {"dp": lax.rem(me + shift, n)},
        )
    mixed = s.mixed[...].reshape(k * T, H)
    for e in range(n):
        go_out[:, e * F : (e + 1) * F] = dot(mixed, s.u_all[e].reshape(k * T, F), TN)

    for shift in range(1, n):
        done(s.gain_all.at[lax.rem(me + n - shift, n)], s.n_r.at[shift - 1])
        done(s.gain_all.at[me], s.n_s.at[shift - 1])
    gain_out[...] = s.gain_all[...]

    @pl.when(sec == 0)
    def _():
        for i in range(d.mb):
            for shift in range(n - 1):
                done(stream.at[pl.ds(i * T, T), pl.ds(0, F)], s.d_s.at[i, shift])

    @pl.when(sec == last)
    def _():
        for i in range(d.mb):
            for shift in range(n - 1):
                done(ograd.at[pl.ds(i * T, T), pl.ds(0, F)], s.g_s.at[i, shift])

    for i, (src, there, dst, here) in enumerate(pieces(1 - core)):
        done(src.at[:, there], s.w_s.at[i])
    for shift in range(1, n):
        done(bias, s.b_s.at[shift - 1])

    def settle(t, carry):
        @pl.when(sec < last)
        def _():
            done(s.z_send.at[t], s.z_s.at[t])

        @pl.when(sec > 0)
        def _():
            done(s.d_send.at[t], s.dz_s.at[t])

        return carry

    lax.fori_loop(0, k, settle, 0)


def weights_kernel(d, normed_in, g_in, gkv_in, go, gain_in, *rest):
    gj_out, go_out, gain_out, gj, out_sems = rest
    n, F, H = d.n, d.F, d.H
    stores = []

    def store(block, out, start, width):
        here = (slice(None), pl.ds(start, width))
        copy = pltpu.make_async_copy(block.at[here], out.at[here], out_sems.at[len(stores)])
        copy.start()
        stores.append(copy)

    for e in range(n):
        store(go, go_out, e * F, F)
    gain_out[...] = jnp.concatenate([gain_in[e] for e in range(n)], axis=1)
    for e in range(n):
        gj[:, e * H : (e + 1) * H] = dot(normed_in[...], g_in[e, :, :H], TN)
        store(gj, gj_out, e * H, H)
    gj[:, n * H :] = dot(normed_in[...], gkv_in[...], TN)
    store(gj, gj_out, n * H, d.W - H)
    for copy in stores:
        copy.wait()


def train_step(d, stream, ograd, masks, gain, wj, wo):
    n, k, T, F, H, W = d.n, d.k, d.T, d.F, d.H, d.W
    o = d.chips - 1
    J = n * H + W - H
    vmem, dma = pltpu.VMEM, pltpu.SemaphoreType.DMA
    each, cross = dma((k,)), dma((o, k))
    scratch = dict(
        wjf=vmem((2 * F, W + o * H), BF16),
        wof=vmem((2 * H, d.chips * F), BF16),
        wj_own=vmem((F, J), BF16),
        wo_own=vmem((H, d.D), BF16),
        wj_turned=vmem((J, F), BF16),
        wo_turned=vmem((d.D, H), BF16),
        bias_all=vmem((n, d.mb, -(-masks.shape[1] // 8) * 8, LANES), F32),
        x_own=vmem((k, T, F), BF16),
        x_sib=vmem((k, T, F), BF16),
        j_own=vmem((k, T, W), F32),
        j_send=vmem((o, k, T, W), BF16),
        j_recv=vmem((o, k, T, W), BF16),
        st_own=vmem((k, 1, LANES), F32),
        st_recv=vmem((o, k, 1, LANES), F32),
        qkv=vmem((k, T, W), BF16),
        r_all=vmem((k, T, LANES), F32),
        probs=vmem((k, H // HEAD_DIM * T, T), F32),
        mixed_sib=vmem((k, T, H), BF16),
        y_own=vmem((k, T, F), F32),
        y_recv=vmem((o, k, T, F), BF16),
        y_send=vmem((o, k, T, F), BF16),
        z_send=vmem((k, T, F), BF16),
        gs_all=vmem((n, k, 1, LANES), F32),
        gm=vmem((k, T, H), BF16),
        d_send=vmem((k, T, F), BF16),
        gain_acc=vmem((8, F), F32),
        gain_all=vmem((n, 1, F), F32),
        w_l=dma((2 * d.chips + 3,)),
        w_s=dma((2 * d.chips + 1,)),
        w_r=dma((2 * d.chips + 1,)),
        b_s=dma((n - 1,)),
        b_r=dma((n - 1,)),
        n_s=dma((n - 1,)),
        n_r=dma((n - 1,)),
        d_s=dma((d.mb, n - 1)),
        g_s=dma((d.mb, n - 1)),
    )
    for name in ("x_r", "u_r", "xs_s", "xs_r", "m_s", "m_r", "z_s", "dz_s"):
        scratch[name] = each
    for name in ("us_s", "us_r", "gs_s", "gs_r"):
        scratch[name] = each
    for name in ("j_s", "j_r", "st_s", "st_r", "y_s", "y_r", "ux_s", "ux_r", "ur_s", "ur_r", "gx_s", "gx_r", "gr_s", "gr_r"):
        scratch[name] = cross
    for name in ("hx_s", "hx_r"):
        scratch[name] = dma((n - 1, k))
    d.names = list(scratch)
    anywhere = pl.BlockSpec(memory_space=pl.ANY)
    inside = pl.BlockSpec(memory_space=pltpu.VMEM)
    rows = k * T
    kept = [(k, T, F), (k, T, H), (n, k, T, W), (k, T, W - H), (n, k, T, F)]
    kept_bytes = 2 * sum(math.prod(shape) for shape in kept) + 4 * H * d.D
    *blocks, go, gain_all = pl.pallas_call(
        functools.partial(step_kernel, d),
        out_shape=[pltpu.VMEM(shape, BF16) for shape in kept]
        + [pltpu.VMEM((H, d.D), F32), jax.ShapeDtypeStruct((n, 1, F), F32)],
        in_specs=[anywhere, anywhere, pl.BlockSpec(memory_space=pltpu.SMEM), inside]
        + [anywhere] * 2,
        out_specs=[inside] * 7,
        scratch_shapes=list(scratch.values()),
        compiler_params=pltpu.CompilerParams(
            collective_id=0, has_side_effects=True, vmem_limit_bytes=VMEM - kept_bytes
        ),
    )(stream, ograd, masks, gain, wj, wo)
    normed, _, g, gkv, _ = blocks
    return pl.pallas_call(
        functools.partial(weights_kernel, d),
        out_shape=[
            jax.ShapeDtypeStruct((F, J), F32),
            jax.ShapeDtypeStruct((H, d.D), F32),
            jax.ShapeDtypeStruct((1, n * F), F32),
        ],
        in_specs=[inside] * 5,
        out_specs=[anywhere] * 2 + [inside],
        scratch_shapes=[vmem((F, J), F32), dma((2 * n + 1,))],
        compiler_params=pltpu.CompilerParams(vmem_limit_bytes=VMEM // 2),
    )(
        normed.reshape(rows, F),
        g.reshape(n, rows, W),
        gkv.reshape(rows, W - H),
        go,
        gain_all,
    )


def body(stream_in, out_grad, mask_blocks, norm_gain, w_joined, w_out):
    n = lax.axis_size("dp")
    wj, wo = w_joined[0], w_out[0]
    mb = mask_blocks.shape[0]
    d = types.SimpleNamespace(
        n=n,
        S=lax.axis_size("section"),
        chips=n // CORES,
        mb=mb,
        k=mb * n,
        T=stream_in.shape[0] // mb,
        F=wj.shape[0],
        D=stream_in.shape[1],
    )
    real = wo.shape[0]
    d.H = -(-real // LANES) * LANES
    d.W = d.H + 2 * HEAD_DIM
    pad = d.H - real
    if pad:
        heads = wj[:, : n * real].reshape(d.F, n, real)
        heads = jnp.pad(heads, ((0, 0), (0, 0), (0, pad))).reshape(d.F, n * d.H)
        wj = jnp.concatenate([heads, wj[:, n * real :]], axis=1)
        wo = jnp.pad(wo, ((0, pad), (0, 0)))
    gj, go, gain = train_step(d, stream_in, out_grad, mask_blocks, norm_gain, wj, wo)
    if pad:
        heads = gj[:, : n * d.H].reshape(d.F, n, d.H)[:, :, :real].reshape(d.F, n * real)
        gj = jnp.concatenate([heads, gj[:, n * d.H :]], axis=1)
        go = go[:real]
    return gj[None], go[None], gain


def solution(mesh):
    return jax.shard_map(
        body,
        mesh=mesh,
        in_specs=(
            P(("groups", "dp"), None),
            P(("groups", "dp"), None),
            P(("groups", "dp"), None, None),
            P("section", None),
            P("section", "dp", None),
            P("section", "dp", None),
        ),
        out_specs=(
            P(("groups", "section"), "dp", None),
            P(("groups", "section"), "dp", None),
            P(("groups", "section"), None),
        ),
        check_vma=False,
    )
```

```python
import functools
import math
import types

import jax
import jax.numpy as jnp
from jax import lax
from jax.experimental import pallas as pl
from jax.experimental.pallas import tpu as pltpu
from jax.sharding import PartitionSpec as P

HEAD_DIM = 64
BLOCK_LEN = 16
LANES = 128
CORES = 2
EPSILON = 1e-05
F32 = jnp.float32
BF16 = jnp.bfloat16
NN = (((1,), (0,)), ((), ()))
NT = (((1,), (1,)), ((), ()))
TN = (((0,), (0,)), ((), ()))

LAG = dict(FA=0, F1=1, F2=3, F3=3, F4=5, BA=0, BR=1, BM=2, B1=2, GR=4, B3=4)
ORDER = ("F2", "GR", "BA", "F1", "BM", "B1", "F4", "F3", "FA", "BR", "B3")
FIRST_BACK = 1
STAGE_GAP = 13
VMEM = 60 << 20


def dot(left, right, dims=NN):
    return lax.dot_general(left, right, dims, preferred_element_type=F32)


def step_kernel(d, stream, ograd, masks, gain, wj, wo, *rest):
    outs, scratch = rest[:7], rest[7:]
    s = types.SimpleNamespace(**dict(zip(d.names, scratch)))
    s.normed, s.mixed, s.g_all, s.gkv, s.u_all, go_out, gain_out = outs
    n, k, T, F, H, W, chips = d.n, d.k, d.T, d.F, d.H, d.W, d.chips
    me = lax.axis_index("dp")
    sec = lax.axis_index("section")
    last = d.S - 1
    chip, core = me // CORES, lax.rem(me, CORES)
    sib = me + 1 - 2 * core
    others = range(1, chips)

    def ahead(kk):
        return lax.rem(chip + kk, chips) * CORES

    def behind(kk):
        return lax.rem(chip + chips - kk, chips) * CORES

    def push(src, dst, send, recv, device):
        pltpu.make_async_remote_copy(
            src_ref=src,
            dst_ref=dst,
            send_sem=send,
            recv_sem=recv,
            device_id=device,
            device_id_type=pl.DeviceIdType.MESH,
        ).start()

    def done(ref, sem):
        pltpu.make_async_copy(ref, ref, sem).wait()

    def cols(index, width):
        return pl.ds(pl.multiple_of(index * width, LANES), width)

    to_sib = {"dp": sib}
    cut = -(-F // (2 * LANES)) * LANES
    parts = [(0, cut), (cut, F - cut)]
    halves = [(h, pl.ds(start, width)) for h, (start, width) in enumerate(parts)]

    def features(index, h):
        start, width = parts[h]
        return pl.ds(pl.multiple_of(index * F + start, LANES), width)

    def column(kk):
        return pl.ds(0, H) if kk == 0 else pl.ds(W + (kk - 1) * H, H)

    def pieces(which):
        out = []
        for kk in range(chips):
            e = ahead(kk) + which
            out.append((wj, cols(e, H), s.wjf, column(kk)))
        out.append((wj, pl.ds(n * H, W - H), s.wjf, pl.ds(H, W - H)))
        for kk in range(chips):
            e = ahead(kk) + which
            out.append((wo, cols(e, F), s.wof, pl.ds(kk * F, F)))
        return out

    loads = []
    for i, (src, there, dst, here) in enumerate(pieces(core)):
        rows = src.shape[0]
        loads.append(
            pltpu.make_async_copy(
                src.at[:, there], dst.at[pl.ds(0, rows), here], s.w_l.at[i]
            )
        )
    loads.append(pltpu.make_async_copy(wj, s.wj_own, s.w_l.at[2 * chips + 1]))
    loads.append(pltpu.make_async_copy(wo, s.wo_own, s.w_l.at[2 * chips + 2]))
    urgent = chips + 1
    for copy in loads[:urgent]:
        copy.start()

    bias = s.bias_all.at[me]
    block_of = lax.broadcasted_iota(jnp.int32, (1, LANES), 1) // BLOCK_LEN
    for m in range(d.mb):
        for q in range(masks.shape[1]):
            hit = block_of == masks[m, q, 0]
            for j in range(1, masks.shape[2]):
                hit = jnp.logical_or(hit, block_of == masks[m, q, j])
            s.bias_all[me, m, q : q + 1, :] = jnp.where(hit, 0.0, -1e30)

    barrier = pltpu.get_barrier_semaphore()

    def greet(device):
        pl.semaphore_signal(
            barrier, inc=1, device_id=device, device_id_type=pl.DeviceIdType.MESH
        )

    for shift in range(1, n):
        greet({"dp": lax.rem(me + shift, n)})

    @pl.when(sec > 0)
    def _():
        greet({"section": sec - 1})

    @pl.when(sec < last)
    def _():
        greet({"section": sec + 1})

    ends = (sec > 0).astype(jnp.int32) + (sec < last).astype(jnp.int32)
    pl.semaphore_wait(barrier, n - 1 + ends)

    def local(src, dst, sem):
        pltpu.make_async_copy(src, dst, sem).start()

    @pl.when(sec == 0)
    def _():
        for i in range(d.mb):
            t = i * n + me
            rows = pl.ds(i * T, T)
            for h, here in halves:
                dst, recv = s.x_own.at[t, :, here], s.x_r.at[h, t]
                local(stream.at[rows, features(me, h)], dst, recv)
                for shift in range(1, n):
                    e = lax.rem(me + shift, n)
                    there = stream.at[rows, features(e, h)]
                    push(there, dst, s.d_s.at[h, i, shift - 1], recv, {"dp": e})

    for i, (src, there, dst, here) in enumerate(pieces(1 - core)):
        rows = src.shape[0]
        push(
            src.at[:, there],
            dst.at[pl.ds(rows, rows), here],
            s.w_s.at[i],
            s.w_r.at[i],
            to_sib,
        )
    for copy in loads[urgent:]:
        copy.start()

    for shift in range(1, n):
        e = lax.rem(me + shift, n)
        push(bias, bias, s.b_s.at[shift - 1], s.b_r.at[shift - 1], {"dp": e})

    @pl.when(sec == last)
    def _():
        for i in range(d.mb):
            t = i * n + me
            rows = pl.ds(i * T, T)
            for h, here in halves:
                recv = s.u_r.at[h, t]
                local(ograd.at[rows, features(me, h)], s.u_all.at[me, t, :, here], recv)
                for shift in range(1, n):
                    e = lax.rem(me + shift, n)
                    there, dst = ograd.at[rows, features(e, h)], s.u_all.at[e, t, :, here]
                    push(there, dst, s.g_s.at[h, i, shift - 1], recv, {"dp": e})

    s.gain_acc[...] = jnp.zeros_like(s.gain_acc)
    def pieces_here(begin, end):
        for i, (src, there, dst, here) in list(enumerate(pieces(core)))[begin:end]:
            rows = src.shape[0]
            loads[i].wait()
            done(dst.at[pl.ds(rows, rows), here], s.w_r.at[i])

    def masks_here():
        for shift in range(1, n):
            done(s.bias_all.at[lax.rem(me + n - shift, n)], s.b_r.at[shift - 1])

    def turn_weights():
        for copy in loads[2 * chips + 1 :]:
            copy.wait()
        s.wo_turned[...] = s.wo_own[...].T
        s.wj_turned[...] = s.wj_own[...].T

    @pl.when(sec > 0)
    def _():
        turn_weights()

    @pl.when(sec == last)
    def _():
        pieces_here(urgent, 2 * chips + 1)

    pieces_here(0, urgent)

    def eye():
        return lax.broadcasted_iota(jnp.int32, (T, LANES), 0) == lax.broadcasted_iota(
            jnp.int32, (T, LANES), 1
        )

    def to_row(column_values):
        return jnp.sum(jnp.where(eye(), column_values, 0.0), axis=0, keepdims=True)

    def to_column(row_values):
        return jnp.sum(
            jnp.where(eye(), jnp.broadcast_to(row_values, (T, LANES)), 0.0), axis=1, keepdims=True
        )

    def low_half(rows):
        return lax.broadcasted_iota(jnp.int32, (rows, LANES), 1) < HEAD_DIM

    def stack_heads(rows):
        low = low_half(T)
        out = []
        for pair in range(H // LANES):
            both = rows[:, pair * LANES : (pair + 1) * LANES]
            out += [jnp.where(low, both, 0.0), jnp.where(low, 0.0, both)]
        return jnp.concatenate(out, axis=0)

    def unstack_heads(rows):
        low = low_half(T)
        out = []
        for pair in range(H // LANES):
            first = rows[2 * pair * T : (2 * pair + 1) * T]
            second = rows[(2 * pair + 1) * T : (2 * pair + 2) * T]
            out.append(jnp.where(low, first, second))
        return jnp.concatenate(out, axis=1)

    def doubled(kv):
        low = low_half(T)
        turned = pltpu.roll(kv, HEAD_DIM, 1)
        return jnp.where(low, kv, turned).astype(BF16), jnp.where(low, turned, kv).astype(BF16)

    peers = [sib] + [ahead(kk) + c for kk in others for c in (core, 1 - core)]
    sources = [sib] + [behind(kk) + c for kk in others for c in (core, 1 - core)]
    g_own = gain[:, cols(me, F)]
    g_sib = gain[:, cols(sib, F)]

    def fa(t):
        for h, here in halves:
            done(s.x_own.at[t, :, here], s.x_r.at[h, t])
        push(s.x_own.at[t], s.x_sib.at[t], s.xs_s.at[t], s.xs_r.at[t], to_sib)

    def f1(t):
        own = s.x_own[t].astype(F32)
        done(s.x_sib.at[t], s.xs_r.at[t])
        beside = s.x_sib[t].astype(F32)
        squares = jnp.sum(own * own, axis=1, keepdims=True) + jnp.sum(
            beside * beside, axis=1, keepdims=True
        )
        part = dot((own * g_own).astype(BF16), s.wjf[:F]) + dot(
            (beside * g_sib).astype(BF16), s.wjf[F:]
        )
        for kk in others:
            s.j_send[kk - 1, t, :, :H] = part[:, W + (kk - 1) * H : W + kk * H].astype(BF16)
            s.j_send[kk - 1, t, :, H:] = part[:, H:W].astype(BF16)
            there = {"dp": ahead(kk) + core}
            at = (kk - 1, t)
            push(s.j_send.at[at], s.j_recv.at[at], s.j_s.at[at], s.j_r.at[at], there)
        s.st_own[t] = to_row(squares)
        s.j_own[t] = part[:, :W]
        for kk in others:
            there = {"dp": ahead(kk) + core}
            at = (kk - 1, t)
            push(s.st_own.at[t], s.st_recv.at[at], s.st_s.at[at], s.st_r.at[at], there)
        done(s.x_own.at[t], s.xs_s.at[t])

    def f2(t):
        total = s.j_own[t]
        squares = s.st_own[t]
        for kk in others:
            at = (kk - 1, t)
            done(s.j_recv.at[at], s.j_r.at[at])
            done(s.st_recv.at[at], s.st_r.at[at])
            total = total + s.j_recv[at].astype(F32)
            squares = squares + s.st_recv[at]
        pl.when(t == 0)(masks_here)
        inv_rms = lax.rsqrt(to_column(squares) / d.D + EPSILON)
        joined = (total * inv_rms).astype(BF16)
        s.qkv[t] = joined
        s.r_all[t] = jnp.broadcast_to(inv_rms, (T, LANES))
        wide = joined.astype(F32)
        queries = stack_heads(wide[:, :H]).astype(BF16)
        kk_rows, vv_rows = doubled(wide[:, H:])
        scores = dot(queries, kk_rows, NT) * HEAD_DIM ** (-0.5)
        blocks = s.bias_all[lax.rem(t, n), t // n]
        rows = [
            jnp.broadcast_to(blocks[b : b + 1, :T], (BLOCK_LEN, T)) for b in range(T // BLOCK_LEN)
        ]
        scores = scores + jnp.concatenate(rows * (H // HEAD_DIM), axis=0)
        exps = jnp.exp(scores - jnp.max(scores, axis=1, keepdims=True))
        probs = exps / jnp.sum(exps, axis=1, keepdims=True)
        s.probs[t] = probs
        s.mixed[t] = unstack_heads(dot(probs.astype(BF16), vv_rows)).astype(BF16)

        @pl.when(sec < last)
        def _():
            push(s.mixed.at[t], s.mixed_sib.at[t], s.m_s.at[t], s.m_r.at[t], to_sib)

        for kk in others:
            at = (kk - 1, t)
            done(s.j_send.at[at], s.j_s.at[at])
            done(s.st_own.at[t], s.st_s.at[at])

    def f3(t):
        @pl.when(sec < last)
        def _():
            done(s.mixed_sib.at[t], s.m_r.at[t])
            pl.when(t == 0)(lambda: pieces_here(urgent, 2 * chips + 1))
            mixed, beside = s.mixed[t], s.mixed_sib[t]
            part = dot(mixed, s.wof[:H, F:]) + dot(beside, s.wof[H:, F:])
            for kk in others:
                s.y_send[kk - 1, t] = part[:, (kk - 1) * F : kk * F].astype(BF16)
                for h, here in halves:
                    push(
                        s.y_send.at[kk - 1, t, :, here],
                        s.y_recv.at[kk - 1, t, :, here],
                        s.y_s.at[h, kk - 1, t],
                        s.y_r.at[h, kk - 1, t],
                        {"dp": ahead(kk) + core},
                    )
            own = dot(mixed, s.wof[:H, :F]) + dot(beside, s.wof[H:, :F])
            s.y_own[t] = own + s.x_own[t].astype(F32)
            done(s.mixed.at[t], s.m_s.at[t])

    def f4(t):
        @pl.when(sec < last)
        def _():
            for h, here in halves:
                total = s.y_own[t, :, here]
                for kk in others:
                    done(s.y_recv.at[kk - 1, t, :, here], s.y_r.at[h, kk - 1, t])
                    total = total + s.y_recv[kk - 1, t, :, here].astype(F32)
                s.z_send[t, :, here] = total.astype(BF16)
                push(
                    s.z_send.at[t, :, here],
                    s.x_own.at[t, :, here],
                    s.z_s.at[h, t],
                    s.x_r.at[h, t],
                    {"section": sec + 1},
                )
            for kk in others:
                for h, here in halves:
                    done(s.y_send.at[kk - 1, t, :, here], s.y_s.at[h, kk - 1, t])

    def ba(t):
        for h, here in halves:
            mine = s.u_all.at[me, t, :, here]
            done(mine, s.u_r.at[h, t])
            for kk in others:
                at = (h, kk - 1, t)
                push(mine, mine, s.ux_s.at[at], s.ux_r.at[at], {"dp": ahead(kk) + core})
        mine = s.u_all.at[me, t]
        push(mine, mine, s.us_s.at[t], s.us_r.at[t], to_sib)

    def br(t):
        for kk in others:
            e = behind(kk) + core
            for h, here in halves:
                done(s.u_all.at[e, t, :, here], s.ux_r.at[h, kk - 1, t])
            block, at = s.u_all.at[e, t], (kk - 1, t)
            push(block, block, s.ur_s.at[at], s.ur_r.at[at], to_sib)

    def bm(t):
        done(s.u_all.at[sib, t], s.us_r.at[t])
        for kk in others:
            done(s.u_all.at[behind(kk) + 1 - core, t], s.ur_r.at[kk - 1, t])
        upstream = jnp.concatenate([s.u_all[e, t] for e in range(n)], axis=1)
        s.gm[t] = dot(upstream, s.wo_turned[...]).astype(BF16)
        done(s.u_all.at[me, t], s.us_s.at[t])
        for kk in others:
            for h, here in halves:
                done(s.u_all.at[me, t, :, here], s.ux_s.at[h, kk - 1, t])
            done(s.u_all.at[behind(kk) + core, t], s.ur_s.at[kk - 1, t])

    def b1(t):
        grads = stack_heads(s.gm[t].astype(F32)).astype(BF16)
        joined = s.qkv[t].astype(F32)
        queries = stack_heads(joined[:, :H]).astype(BF16)
        kk_rows, vv_rows = doubled(joined[:, H:])
        probs = s.probs[t]
        grad_probs = dot(grads, vv_rows, NT)
        inner = jnp.sum(probs * grad_probs, axis=1, keepdims=True)
        grad_scores = (probs * (grad_probs - inner) * HEAD_DIM ** (-0.5)).astype(BF16)
        grad_values = dot(probs.astype(BF16), grads, TN)
        grad_keys = dot(grad_scores, queries, TN)
        grad_queries = unstack_heads(dot(grad_scores, kk_rows))
        grad_kv = jnp.where(
            low_half(T),
            grad_keys + pltpu.roll(grad_keys, HEAD_DIM, 1),
            grad_values + pltpu.roll(grad_values, HEAD_DIM, 1),
        )
        message = jnp.concatenate([grad_queries, grad_kv], axis=1)
        s.g_all[me, t] = message.astype(BF16)
        mine, stat = s.g_all.at[me, t], s.gs_all.at[me, t]
        for kk in others:
            at = (kk - 1, t)
            push(mine, mine, s.gx_s.at[at], s.gx_r.at[at], {"dp": ahead(kk) + core})
        push(mine, mine, s.gs_s.at[t], s.gs_r.at[t], to_sib)
        s.gs_all[me, t] = to_row(jnp.sum(message * joined, axis=1, keepdims=True))
        for shift, e in enumerate(peers):
            at = (shift, t)
            push(stat, stat, s.hx_s.at[at], s.hx_r.at[at], {"dp": e})

    def gr(t):
        for kk in others:
            at = (kk - 1, t)
            block = s.g_all.at[behind(kk) + core, t]
            done(block, s.gx_r.at[at])
            push(block, block, s.gr_s.at[at], s.gr_r.at[at], to_sib)

    def b3(t):
        done(s.g_all.at[sib, t], s.gs_r.at[t])
        for kk in others:
            done(s.g_all.at[behind(kk) + 1 - core, t], s.gr_r.at[kk - 1, t])
        for shift, e in enumerate(sources):
            done(s.gs_all.at[e, t], s.hx_r.at[shift, t])
        blocks = [s.g_all[e, t] for e in range(n)]
        grad_kv = functools.reduce(lambda a, b: a + b, [b[:, H:].astype(F32) for b in blocks])
        grad_kv = grad_kv.astype(BF16)
        rows = jnp.concatenate([b[:, :H] for b in blocks] + [grad_kv], axis=1)
        grad_normed = dot(rows, s.wj_turned[...])
        stat = functools.reduce(lambda a, b: a + b, [s.gs_all[e, t] for e in range(n)])
        inv_rms = s.r_all[t][:, :1]
        wide = s.x_own[t].astype(F32)
        scaled = wide * inv_rms

        @pl.when(sec > 0)
        def _():
            mean = to_column(stat) / d.D
            down = s.u_all[me, t].astype(F32) + inv_rms * (g_own * grad_normed - scaled * mean)
            s.d_send[t] = down.astype(BF16)
            for h, here in halves:
                push(
                    s.d_send.at[t, :, here],
                    s.u_all.at[me, t, :, here],
                    s.dz_s.at[h, t],
                    s.u_r.at[h, t],
                    {"section": sec - 1},
                )

        s.normed[t] = (scaled * g_own).astype(BF16)
        s.gain_acc[...] += jnp.sum((grad_normed * scaled).reshape(T // 8, 8, F), axis=0)
        s.gkv[t] = grad_kv

        done(s.g_all.at[me, t], s.gs_s.at[t])
        for kk in others:
            done(s.g_all.at[me, t], s.gx_s.at[kk - 1, t])
            done(s.g_all.at[behind(kk) + core, t], s.gr_s.at[kk - 1, t])
        for shift in range(n - 1):
            done(s.gs_all.at[me, t], s.hx_s.at[shift, t])

    @pl.when(sec == last)
    def _():
        for phase in (ba, br, bm):
            lax.fori_loop(0, k, lambda t, c, phase=phase: (phase(t), c)[1], 0)

    phases = dict(FA=fa, F1=f1, F2=f2, F3=f3, F4=f4, BA=ba, BR=br, BM=bm, B1=b1, GR=gr, B3=b3)
    gap = jnp.minimum(FIRST_BACK + STAGE_GAP * (last - sec), k + LAG["F4"])

    def step(now, carry):
        pl.when(jnp.logical_and(sec == 0, now == k))(turn_weights)
        for name in ORDER:
            t = now - LAG[name] - (gap if name[0] != "F" else 0)
            run = jnp.logical_and(t >= 0, t < k)
            if name in ("BA", "BR", "BM"):
                run = jnp.logical_and(run, sec < last)

            @pl.when(run)
            def _(name=name, t=t):
                phases[name](t)

        return carry

    lax.fori_loop(0, k + jnp.maximum(gap + LAG["B3"], LAG["F4"]), step, 0)

    s.gain_all[me] = jnp.sum(s.gain_acc[...], axis=0, keepdims=True)
    for shift in range(1, n):
        push(
            s.gain_all.at[me],
            s.gain_all.at[me],
            s.n_s.at[shift - 1],
            s.n_r.at[shift - 1],
            {"dp": lax.rem(me + shift, n)},
        )
    mixed = s.mixed[...].reshape(k * T, H)
    for e in range(n):
        go_out[:, e * F : (e + 1) * F] = dot(mixed, s.u_all[e].reshape(k * T, F), TN)

    for shift in range(1, n):
        done(s.gain_all.at[lax.rem(me + n - shift, n)], s.n_r.at[shift - 1])
        done(s.gain_all.at[me], s.n_s.at[shift - 1])
    gain_out[...] = s.gain_all[...]

    @pl.when(sec == 0)
    def _():
        for i in range(d.mb):
            for shift in range(n - 1):
                for h, here in halves:
                    done(stream.at[pl.ds(i * T, T), here], s.d_s.at[h, i, shift])

    @pl.when(sec == last)
    def _():
        for i in range(d.mb):
            for shift in range(n - 1):
                for h, here in halves:
                    done(ograd.at[pl.ds(i * T, T), here], s.g_s.at[h, i, shift])

    for i, (src, there, dst, here) in enumerate(pieces(1 - core)):
        done(src.at[:, there], s.w_s.at[i])
    for shift in range(1, n):
        done(bias, s.b_s.at[shift - 1])

    def settle(t, carry):
        @pl.when(sec < last)
        def _():
            for h, here in halves:
                done(s.z_send.at[t, :, here], s.z_s.at[h, t])

        @pl.when(sec > 0)
        def _():
            for h, here in halves:
                done(s.d_send.at[t, :, here], s.dz_s.at[h, t])

        return carry

    lax.fori_loop(0, k, settle, 0)


def weights_kernel(d, normed_in, g_in, gkv_in, go, gain_in, *rest):
    gj_out, go_out, gain_out, gj, out_sems = rest
    n, F, H = d.n, d.F, d.H
    stores = []

    def store(block, out, start, width):
        here = (slice(None), pl.ds(start, width))
        copy = pltpu.make_async_copy(block.at[here], out.at[here], out_sems.at[len(stores)])
        copy.start()
        stores.append(copy)

    for e in range(n):
        store(go, go_out, e * F, F)
    gain_out[...] = jnp.concatenate([gain_in[e] for e in range(n)], axis=1)
    for e in range(n):
        gj[:, e * H : (e + 1) * H] = dot(normed_in[...], g_in[e, :, :H], TN)
        store(gj, gj_out, e * H, H)
    gj[:, n * H :] = dot(normed_in[...], gkv_in[...], TN)
    store(gj, gj_out, n * H, d.W - H)
    for copy in stores:
        copy.wait()


def train_step(d, stream, ograd, masks, gain, wj, wo):
    n, k, T, F, H, W = d.n, d.k, d.T, d.F, d.H, d.W
    o = d.chips - 1
    J = n * H + W - H
    vmem, dma = pltpu.VMEM, pltpu.SemaphoreType.DMA
    each, cross = dma((k,)), dma((o, k))
    scratch = dict(
        wjf=vmem((2 * F, W + o * H), BF16),
        wof=vmem((2 * H, d.chips * F), BF16),
        wj_own=vmem((F, J), BF16),
        wo_own=vmem((H, d.D), BF16),
        wj_turned=vmem((J, F), BF16),
        wo_turned=vmem((d.D, H), BF16),
        bias_all=vmem((n, d.mb, -(-masks.shape[1] // 8) * 8, LANES), F32),
        x_own=vmem((k, T, F), BF16),
        x_sib=vmem((k, T, F), BF16),
        j_own=vmem((k, T, W), F32),
        j_send=vmem((o, k, T, W), BF16),
        j_recv=vmem((o, k, T, W), BF16),
        st_own=vmem((k, 1, LANES), F32),
        st_recv=vmem((o, k, 1, LANES), F32),
        qkv=vmem((k, T, W), BF16),
        r_all=vmem((k, T, LANES), F32),
        probs=vmem((k, H // HEAD_DIM * T, T), F32),
        mixed_sib=vmem((k, T, H), BF16),
        y_own=vmem((k, T, F), F32),
        y_recv=vmem((o, k, T, F), BF16),
        y_send=vmem((o, k, T, F), BF16),
        z_send=vmem((k, T, F), BF16),
        gs_all=vmem((n, k, 1, LANES), F32),
        gm=vmem((k, T, H), BF16),
        d_send=vmem((k, T, F), BF16),
        gain_acc=vmem((8, F), F32),
        gain_all=vmem((n, 1, F), F32),
        w_l=dma((2 * d.chips + 3,)),
        w_s=dma((2 * d.chips + 1,)),
        w_r=dma((2 * d.chips + 1,)),
        b_s=dma((n - 1,)),
        b_r=dma((n - 1,)),
        n_s=dma((n - 1,)),
        n_r=dma((n - 1,)),
        d_s=dma((2, d.mb, n - 1)),
        g_s=dma((2, d.mb, n - 1)),
    )
    for name in ("xs_s", "xs_r", "m_s", "m_r"):
        scratch[name] = each
    for name in ("x_r", "u_r", "z_s", "dz_s"):
        scratch[name] = dma((2, k))
    for name in ("y_s", "y_r", "ux_s", "ux_r"):
        scratch[name] = dma((2, o, k))
    for name in ("us_s", "us_r", "gs_s", "gs_r"):
        scratch[name] = each
    for name in ("j_s", "j_r", "st_s", "st_r", "ur_s", "ur_r", "gx_s", "gx_r", "gr_s", "gr_r"):
        scratch[name] = cross
    for name in ("hx_s", "hx_r"):
        scratch[name] = dma((n - 1, k))
    d.names = list(scratch)
    anywhere = pl.BlockSpec(memory_space=pl.ANY)
    inside = pl.BlockSpec(memory_space=pltpu.VMEM)
    rows = k * T
    kept = [(k, T, F), (k, T, H), (n, k, T, W), (k, T, W - H), (n, k, T, F)]
    kept_bytes = 2 * sum(math.prod(shape) for shape in kept) + 4 * H * d.D
    *blocks, go, gain_all = pl.pallas_call(
        functools.partial(step_kernel, d),
        out_shape=[pltpu.VMEM(shape, BF16) for shape in kept]
        + [pltpu.VMEM((H, d.D), F32), jax.ShapeDtypeStruct((n, 1, F), F32)],
        in_specs=[anywhere, anywhere, pl.BlockSpec(memory_space=pltpu.SMEM), inside]
        + [anywhere] * 2,
        out_specs=[inside] * 7,
        scratch_shapes=list(scratch.values()),
        compiler_params=pltpu.CompilerParams(
            collective_id=0, has_side_effects=True, vmem_limit_bytes=VMEM - kept_bytes
        ),
    )(stream, ograd, masks, gain, wj, wo)
    normed, _, g, gkv, _ = blocks
    return pl.pallas_call(
        functools.partial(weights_kernel, d),
        out_shape=[
            jax.ShapeDtypeStruct((F, J), F32),
            jax.ShapeDtypeStruct((H, d.D), F32),
            jax.ShapeDtypeStruct((1, n * F), F32),
        ],
        in_specs=[inside] * 5,
        out_specs=[anywhere] * 2 + [inside],
        scratch_shapes=[vmem((F, J), F32), dma((2 * n + 1,))],
        compiler_params=pltpu.CompilerParams(vmem_limit_bytes=VMEM // 2),
    )(
        normed.reshape(rows, F),
        g.reshape(n, rows, W),
        gkv.reshape(rows, W - H),
        go,
        gain_all,
    )


def body(stream_in, out_grad, mask_blocks, norm_gain, w_joined, w_out):
    n = lax.axis_size("dp")
    wj, wo = w_joined[0], w_out[0]
    mb = mask_blocks.shape[0]
    d = types.SimpleNamespace(
        n=n,
        S=lax.axis_size("section"),
        chips=n // CORES,
        mb=mb,
        k=mb * n,
        T=stream_in.shape[0] // mb,
        F=wj.shape[0],
        D=stream_in.shape[1],
    )
    real = wo.shape[0]
    d.H = -(-real // LANES) * LANES
    d.W = d.H + 2 * HEAD_DIM
    pad = d.H - real
    if pad:
        heads = wj[:, : n * real].reshape(d.F, n, real)
        heads = jnp.pad(heads, ((0, 0), (0, 0), (0, pad))).reshape(d.F, n * d.H)
        wj = jnp.concatenate([heads, wj[:, n * real :]], axis=1)
        wo = jnp.pad(wo, ((0, pad), (0, 0)))
    gj, go, gain = train_step(d, stream_in, out_grad, mask_blocks, norm_gain, wj, wo)
    if pad:
        heads = gj[:, : n * d.H].reshape(d.F, n, d.H)[:, :, :real].reshape(d.F, n * real)
        gj = jnp.concatenate([heads, gj[:, n * d.H :]], axis=1)
        go = go[:real]
    return gj[None], go[None], gain


def solution(mesh):
    return jax.shard_map(
        body,
        mesh=mesh,
        in_specs=(
            P(("groups", "dp"), None),
            P(("groups", "dp"), None),
            P(("groups", "dp"), None, None),
            P("section", None),
            P("section", "dp", None),
            P("section", "dp", None),
        ),
        out_specs=(
            P(("groups", "section"), "dp", None),
            P(("groups", "section"), "dp", None),
            P(("groups", "section"), None),
        ),
        check_vma=False,
    )
```
